32 devices in a mesh: grp: 2 (over x), blk: 16 (over z, y, core).
Axes of the slice: x: 2, y: 2, z: 4, core: 2. Of those that a mesh axis runs over, the one named last changes fastest.
Arguments:
- queries: bfloat16 [32, 5120], P(('grp', 'blk')), parts along dimension 0, may hold values from -128 to 128
- home_device: int32 [8], P('grp'), parts along dimension 0, may hold values from 0 to 15, as said below
- lengths: int32 [8], P('grp'), parts along dimension 0, may hold values from 256 to 2048, as said below
- key_cache: bfloat16 [8, 2048, 1024], P('grp', 'blk'), parts along dimension 0, may hold values from -8 to 8
- value_cache: bfloat16 [8, 2048, 1024], P('grp', 'blk'), parts along dimension 0, may hold values from -6 to 6
- residual: bfloat16 [8, 5120], P('grp', 'blk'), parts along dimension 0, may hold values from -4 to 4
- out_weight: bfloat16 [5120, 5120], P('blk'), may hold values from -0.125 to 0.125
- ffn_gain: float32 [5120], replicated, may hold values from 0.5 to 1.5
- gate_weight: bfloat16 [5120, 27648], P(None, 'blk'), may hold values from -0.078125 to 0.078125
- up_weight: bfloat16 [5120, 27648], P(None, 'blk'), may hold values from -0.078125 to 0.078125
- down_weight: bfloat16 [27648, 5120], P('blk'), may hold values from -0.0546875 to 0.0546875
- query_gain: float32 [5120], replicated, may hold values from 0.5 to 1.5
- query_weight: bfloat16 [5120, 5120], P(None, 'blk'), may hold values from -0.078125 to 0.078125
- query_bias: float32 [5120], P('blk'), may hold values from -3 to 3
Outputs:
- hidden_out: bfloat16 [8, 5120], P('grp', 'blk'), parts along dimension 0
- next_queries: bfloat16 [32, 5120], P(('grp', 'blk')), parts along dimension 0
The draws below stay inside these ranges and needn't reach their ends.
There are 2 independent parts, one for each index of `grp`. The reference program is written for one: setup_inputs(seed, part) draws one part's arguments, and reference() takes and returns one part's arrays. A program takes and returns all parts, laid end to end along the dimension named above; an argument that names none is the same for every part. Nothing has to cross between parts.
Inputs may be any that keep to these rules, and one draw needn't show every extreme that they name: `home_device`: distinct device indices below 16; the last device is home to one sequence in every draw; rows of queries at devices that are home to no sequence are not read. `lengths`: one sequence of every draw has the full 2048 positions.
All inputs are finite; a program needn't handle non-finite values.
Results may differ from the reference program's by a relative error of at most 0.018.
Values may be sent and summed in bfloat16 or wider, within the bound.
A program may use at most 128 MiB of HBM per device.

```python
import jax
import jax.numpy as jnp
from jax import lax

D = 5120
HQ = 40
KVH = 8
HEAD = 128
FF = 27648
SEQS = 4
SHARDS = 16
CTX = 2048


def layout(key):
    folded = jax.random.fold_in(key, 4409)
    subkeys = jax.random.split(folded, 7)
    picked = jax.random.permutation(subkeys[0], SHARDS)[:SEQS].astype(jnp.int32)
    has_last = jnp.any(picked == SHARDS - 1)
    last_slot = jax.random.randint(subkeys[6], (), 0, SEQS)
    forced = jnp.where(jnp.arange(SEQS) == last_slot, SHARDS - 1, picked)
    homes_drawn = jnp.where(has_last, picked, forced).astype(jnp.int32)
    sampled = jax.random.randint(subkeys[1], (SEQS,), CTX // 8, CTX + 1)
    longest = jax.random.randint(subkeys[2], (), 0, SEQS)
    lengths = jnp.where(jnp.arange(SEQS) == longest, CTX, sampled).astype(jnp.int32)
    return (homes_drawn, lengths)


def draw_home_device(key, part):
    return layout(key)[0]


def draw_lengths(key, part):
    return layout(key)[1]


def draw_queries(key, part):
    jitter_key, scale_key = jax.random.split(jax.random.fold_in(key, 811), 2)
    jitter = jnp.clip(jax.random.normal(jitter_key, (SHARDS, HQ, HEAD), jnp.float32), -6.0, 6.0)
    head_scale = jnp.exp(jax.random.uniform(scale_key, (SHARDS, HQ, 1), jnp.float32, jnp.log(0.3), jnp.log(3.0)))
    drawn = (jitter * head_scale).reshape(SHARDS, HQ * HEAD)
    return drawn.astype(jnp.bfloat16)


def draw_key_cache(key, part):
    jitter = jnp.clip(jax.random.normal(jax.random.fold_in(key, 977), (SEQS, CTX, KVH, HEAD), jnp.float32), -6.0, 6.0)
    return jitter.reshape(SEQS, CTX, KVH * HEAD).astype(jnp.bfloat16)


def strengthened(drawn, key, source, target, parts, factor):
    def block_of(axis_at):
        return (jnp.arange(drawn.shape[axis_at]) // (drawn.shape[axis_at] // parts)).reshape((-1,) + (1,) * (drawn.ndim - 1 - axis_at))

    one_side = jax.random.permutation(key, parts)[block_of(target)]
    far = (block_of(target) + parts // 2) % parts
    return jnp.where((block_of(source) == one_side) | (block_of(source) == far), factor * drawn, drawn)


def steps_of(rng, extent, cuts, smallest, largest):
    factor_of = 1.0
    for dim, shards_of in cuts:
        heights = jax.random.uniform(jax.random.fold_in(jax.random.fold_in(rng, 6), dim), (shards_of,), jnp.float32, smallest / len(cuts), largest / len(cuts))
        factor_of = factor_of * jnp.repeat(jnp.exp(heights), extent[dim] // shards_of).reshape((-1,) + (1,) * (len(extent) - 1 - dim))
    return factor_of


def gaussian(own_key, extent, deviation, limit, pieces=(), kind=jnp.bfloat16):
    result = deviation * jax.random.normal(own_key, extent, jnp.float32)
    if pieces:
        result = result * steps_of(own_key, extent, pieces, -0.22, 0.18)
    return jnp.clip(result, -limit, limit).astype(kind)


def heavy_noise(rng, dims, scale, bound, cuts, heavy, kind=jnp.bfloat16):
    entries = scale * jax.random.normal(rng, dims, jnp.float32)
    if cuts:
        entries = entries * steps_of(rng, dims, cuts, -0.22, 0.18)
    return jnp.clip(strengthened(entries, jax.random.fold_in(rng, 3), *heavy), -bound, bound).astype(kind)


def setup_inputs(seed: int = 0, part: int = 0) -> dict:
    key_of = jax.random.split(jax.random.key(seed), 15)
    part_keys = jax.random.split(jax.random.fold_in(key_of[14], part), 15)
    return {
        "queries": draw_queries(jax.random.fold_in(jax.random.fold_in(key_of[14], part), 71), part),
        "home_device": draw_home_device(jax.random.fold_in(jax.random.fold_in(key_of[14], part), 71), part),
        "lengths": draw_lengths(jax.random.fold_in(jax.random.fold_in(key_of[14], part), 71), part),
        "key_cache": draw_key_cache(jax.random.fold_in(jax.random.fold_in(key_of[14], part), 71), part),
        "value_cache": gaussian(part_keys[4], (SEQS, CTX, KVH * HEAD), 1.0, 6.0, ((1, 16),)),
        "residual": gaussian(part_keys[5], (SEQS, D), 0.3, 4.0, ((1, 16),)),
        "out_weight": heavy_noise(key_of[6], (D, D), D ** -0.5, 0.125, ((0, 16),), (0, 1, 16, 2.0)),
        "ffn_gain": jnp.clip(1.0 + 0.1 * jax.random.normal(key_of[7], (D,), jnp.float32), 0.5, 1.5),
        "gate_weight": gaussian(key_of[8], (D, FF), D ** -0.5, 0.078125, ((1, 16),)),
        "up_weight": gaussian(key_of[9], (D, FF), D ** -0.5, 0.078125, ((1, 16),)),
        "down_weight": heavy_noise(key_of[10], (FF, D), FF ** -0.5, 0.0546875, ((0, 16),), (0, 1, 16, 2.0)),
        "query_gain": jnp.clip(1.0 + 0.1 * jax.random.normal(key_of[11], (D,), jnp.float32), 0.5, 1.5),
        "query_weight": gaussian(key_of[12], (D, D), D ** -0.5, 0.078125, ((1, 16),)),
        "query_bias": gaussian(key_of[13], (D,), 0.5, 3.0, ((0, 16),), jnp.float32),
    }


def attend(packed):
    query_row, key_rows, value_rows, length = packed
    group_size = HQ // KVH
    query_heads = query_row.astype(jnp.float32).reshape(KVH, group_size, HEAD)
    key_heads = key_rows.astype(jnp.float32).reshape(CTX, KVH, HEAD)
    value_heads = value_rows.astype(jnp.float32).reshape(CTX, KVH, HEAD)
    scores = jnp.einsum('kgd,tkd->kgt', query_heads, key_heads) * HEAD ** (-0.5)
    usable = (jnp.arange(CTX) < length)[None, None, :]
    masked = jnp.where(usable, scores, -1e+30)
    highest = lax.optimization_barrier(jnp.max(masked, axis=-1, keepdims=True))
    raised = jnp.where(usable, jnp.exp(masked - highest), 0.0)
    totals = lax.optimization_barrier(jnp.sum(raised, axis=-1))
    weights = lax.optimization_barrier(raised.astype(jnp.bfloat16)).astype(jnp.float32)
    summed = jnp.einsum('kgt,tkd->kgd', weights, value_heads)
    return (summed / totals[..., None]).reshape(D).astype(jnp.bfloat16)

def rms_scale(carried, gain_row):
    widened = carried.astype(jnp.float32)
    spread = lax.optimization_barrier(jnp.mean(widened * widened, axis=-1, keepdims=True))
    return (widened * lax.rsqrt(spread + 1e-06) * gain_row).astype(jnp.bfloat16)

def reference(queries, home_device, lengths, key_cache, value_cache, residual, out_weight, ffn_gain, gate_weight, up_weight, down_weight, query_gain, query_weight, query_bias):
    seq_rows = queries[home_device]
    context = lax.map(attend, (seq_rows, key_cache, value_cache, lengths))
    carried = (residual.astype(jnp.float32) + jnp.dot(context, out_weight, preferred_element_type=jnp.float32)).astype(jnp.bfloat16)
    ffn_input = rms_scale(carried, ffn_gain)
    gate_part = jnp.dot(ffn_input, gate_weight, preferred_element_type=jnp.float32)
    up_part = jnp.dot(ffn_input, up_weight, preferred_element_type=jnp.float32)
    activated = (jax.nn.silu(gate_part) * up_part).astype(jnp.bfloat16)
    hidden_out = (carried.astype(jnp.float32) + jnp.dot(activated, down_weight, preferred_element_type=jnp.float32)).astype(jnp.bfloat16)
    query_input = rms_scale(hidden_out, query_gain)
    fresh_query = (jnp.dot(query_input, query_weight, preferred_element_type=jnp.float32) + query_bias).astype(jnp.bfloat16)
    next_queries = jnp.zeros((SHARDS, D), jnp.bfloat16).at[home_device].set(fresh_query)
    return (hidden_out, next_queries)
```

```python
import functools
import math

import jax
import jax.numpy as jnp
from jax import lax
from jax.experimental import pallas as pl
from jax.experimental.pallas import tpu as pltpu
from jax.sharding import PartitionSpec as P

HQ = 40
KVH = 8
HEAD = 128
LANES = 128
GROUP = HQ // KVH
MESH = pl.DeviceIdType.MESH
F32 = jnp.float32
BF16 = jnp.bfloat16

ASK, MERGE, SUM_A, ROW_A, SUM_B, ROW_B, HOME = range(7)


class Plan:
    def __init__(self, n, width, wanted):
        self.n = n
        self.width = width
        self.feat = width // n
        unit = math.lcm(self.feat, LANES)
        self.chunk = unit
        while self.chunk * 2 <= wanted and width % (self.chunk * 2) == 0:
            self.chunk *= 2
        self.chunks = width // self.chunk
        self.per = self.chunk // self.feat
        self.tiles = self.chunk // LANES
        starts = [j * self.feat for j in range(self.per)]
        self.span = max(pl.cdiv(s % LANES + self.feat, LANES) for s in starts)
        self.clamped = any(s // LANES > self.tiles - self.span for s in starts)
        self.win = self.span * LANES
        self.first = [min(s // LANES, self.tiles - self.span) for s in starts]
        self.offsets = sorted({s - f * LANES for s, f in zip(starts, self.first)})

    def first_of(self, j):
        first = (j * self.feat) // LANES
        return jnp.minimum(first, self.tiles - self.span) if self.clamped else first


def dot_rows(left, right):
    return lax.dot_general(
        left, right, (((1,), (1,)), ((), ())), preferred_element_type=F32
    )


def kernel(
    plan,
    share,
    groups,
    home_hbm,
    length_hbm,
    query_bias,
    queries,
    residual_hbm,
    ffn_gain_hbm,
    query_gain_hbm,
    key_hbm,
    value_hbm,
    out_hbm,
    gate_hbm,
    up_hbm,
    down_hbm,
    query_hbm,
    hidden_out,
    next_out,
    home,
    length,
    residual,
    ffn_gain,
    query_gain,
    keys,
    values,
    out_w,
    gate_w,
    up_w,
    down_w,
    query_w,
    asked,
    heads,
    flat,
    stats,
    merge_send,
    merge_recv,
    sum_a_send,
    sum_a_recv,
    row_a_send,
    row_a_recv,
    sum_b_send,
    sum_b_recv,
    row_b_send,
    row_b_recv,
    home_send,
    home_recv,
    shifted,
    taken,
    wide,
    load_sem,
    send_sem,
    recv_sem,
):
    n, feat, width = plan.n, plan.feat, plan.width
    chunk, chunks, per, tiles = plan.chunk, plan.chunks, plan.per, plan.tiles
    win = plan.win
    me = lax.axis_index("blk")
    grp = lax.axis_index("grp")
    seqs = residual.shape[0]
    span = keys.shape[1]
    my_chunk = me // per
    my_place = lax.rem(me, per)
    hidden = gate_w.shape[0]
    shard = grp if share > 1 else 0
    half = pl.ds(pl.multiple_of(shard * hidden, 16), hidden)

    def load(src, dst, i):
        return pltpu.make_async_copy(src, dst, load_sem.at[i])

    loads = [
        load(src, dst, i)
        for i, (src, dst) in enumerate(
            (
                (queries, asked.at[me]),
                (home_hbm, home),
                (length_hbm, length),
                (key_hbm, keys),
                (value_hbm, values),
                (residual_hbm, residual),
                (out_hbm, out_w),
                (ffn_gain_hbm, ffn_gain),
                (gate_hbm.at[half], gate_w),
                (up_hbm.at[half], up_w),
                (down_hbm.at[half], down_w),
                (query_gain_hbm, query_gain),
                (query_hbm, query_w),
            )
        )
    ]
    ASKED, HOMES, LENGTHS, KEYS, VALUES, REST, OUT, GAIN_A, GATE, UP, DOWN, GAIN_B, QUERY = range(13)

    def each(low, high, action):
        def body(i, carry):
            action(i)
            return carry

        lax.fori_loop(low, high, body, 0, unroll=high - low <= 40)

    barrier = pltpu.get_barrier_semaphore()

    def greet(off):
        pl.semaphore_signal(
            barrier,
            inc=1,
            device_id={
                "grp": lax.rem(grp + off // n, share) if share > 1 else grp,
                "blk": lax.rem(me + off, n),
            },
            device_id_type=MESH,
        )

    loads[ASKED].start()
    each(1, n * share, greet)
    for one in loads[1:]:
        one.start()

    def remote(phase, source, target, sem, g, peer):
        pltpu.make_async_remote_copy(
            src_ref=source,
            dst_ref=target,
            send_sem=send_sem.at[phase],
            recv_sem=sem,
            device_id={"grp": g, "blk": peer},
            device_id_type=MESH,
        ).start()

    def start(phase, source, target):
        def send(off):
            peer = lax.rem(me + off, n)
            remote(phase, source(peer), target.at[me], recv_sem.at[phase, 0], grp, peer)

        each(1, n, send)

    def await_bytes(sem, target, count):
        part = target.at[pl.ds(0, count)]
        pltpu.make_async_copy(part, part, sem).wait()

    def slot(parts, g, peer):
        if parts == 1:
            return peer
        return (peer // per) * (parts * per) + g * per + lax.rem(peer, per)

    def reach(c, parts, action):
        at = lax.rem(my_chunk + c, chunks)

        def one(i):
            g = lax.rem(grp + i // per, parts) if parts > 1 else grp
            j = lax.rem(my_place + i, per)
            action(g, at * per + j, j, at)

        each(1 if c == 0 else 0, parts * per, one)

    heads[...] = jnp.zeros_like(heads)
    stats[...] = jnp.zeros_like(stats)
    shifted[...] = jnp.zeros_like(shifted)

    my_first = plan.first_of(my_place)
    offset = my_place * feat - my_first * LANES
    lane = lax.broadcasted_iota(jnp.int32, (seqs, win), 1)
    mine = (lane >= offset) & (lane < offset + feat)

    def narrow(value):
        taken[...] = value
        found = taken[:, plan.offsets[0] : plan.offsets[0] + feat]
        for o in plan.offsets[1:]:
            found = jnp.where(offset == o, taken[:, o : o + feat], found)
        return found

    def widen(value):
        for i, o in enumerate(plan.offsets):
            shifted[i, :, o : o + feat] = value
        found = shifted[0]
        for i, o in enumerate(plan.offsets[1:]):
            found = jnp.where(offset == o, shifted[i + 1], found)
        return found

    loads[ASKED].wait()
    pl.semaphore_wait(barrier, n * share - 1)
    start(ASK, lambda peer: asked.at[me], asked)
    loads[HOMES].wait()
    loads[LENGTHS].wait()
    loads[REST].wait()
    resting = widen(residual[...].astype(F32))
    loads[KEYS].wait()
    loads[VALUES].wait()

    pad = 8
    rows = KVH * pad
    position = me * span + lax.broadcasted_iota(jnp.int32, (rows, span), 1)
    at_row = lax.broadcasted_iota(jnp.int32, (rows, LANES), 0)
    at_lane = lax.broadcasted_iota(jnp.int32, (rows, LANES), 1)
    row_head = (at_row // pad) * GROUP + lax.rem(at_row, pad)
    real = lax.rem(at_row, pad) < GROUP
    await_bytes(recv_sem.at[ASK, 0], asked, n - 1)
    for s in range(seqs):
        line = asked[home[s]].astype(F32)
        for h in range(HQ):
            heads[s, h // GROUP, pl.ds(h % GROUP, 1), :] = line[:, h * HEAD : (h + 1) * HEAD]
        scores = jnp.concatenate(
            [
                dot_rows(heads[s, k].astype(BF16), keys[s, :, k * HEAD : (k + 1) * HEAD])
                for k in range(KVH)
            ],
            axis=0,
        ) * HEAD ** (-0.5)
        allowed = position < length[s]
        masked = jnp.where(allowed, scores, -1e30)
        peak = jnp.max(masked, axis=1, keepdims=True).astype(BF16).astype(F32)
        raised = jnp.where(allowed, jnp.exp(masked - peak), 0.0)
        total = jnp.sum(raised, axis=1, keepdims=True)
        high = total.astype(BF16).astype(F32)
        for k in range(KVH):
            mixed = jnp.dot(
                raised[k * pad : (k + 1) * pad].astype(BF16),
                values[s, :, k * HEAD : (k + 1) * HEAD],
                preferred_element_type=F32,
            )
            for g in range(GROUP):
                h = k * GROUP + g
                flat[pl.ds(s, 1), h * HEAD : (h + 1) * HEAD] = mixed[g : g + 1]
        spread = jnp.where(at_lane == row_head, peak, 0.0)
        spread = spread + jnp.where(at_lane == row_head + HQ, high, 0.0)
        spread = spread + jnp.where(at_lane == row_head + 2 * HQ, total - high, 0.0)
        stats[pl.ds(s, 1), :] = jnp.sum(jnp.where(real, spread, 0.0), axis=0, keepdims=True)

    noted = stats[...]
    for d in range(n):
        tile = (d // per) * tiles + plan.first[d % per]
        merge_send[d, :, 0:win] = flat[:, tile * LANES : tile * LANES + win].astype(BF16)
        rolled = pltpu.roll(noted, (LANES - tile) % LANES, 1) if tile else noted
        merge_send[d, :, win : win + LANES] = rolled[0:seqs].astype(BF16)
    start(MERGE, lambda peer: merge_send.at[peer], merge_recv)
    merge_recv[me] = merge_send[me]
    loads[OUT].wait()
    await_bytes(recv_sem.at[MERGE, 0], merge_recv, n - 1)

    stat = merge_recv[:, :, win : win + LANES].astype(F32)
    scale = jnp.exp(stat - jnp.max(stat, axis=0, keepdims=True))
    blended = []
    for t in range(plan.span):
        own = scale[:, :, t : t + 1]
        whole = stat[:, :, HQ + t : HQ + t + 1] + stat[:, :, 2 * HQ + t : 2 * HQ + t + 1]
        factor = own / jnp.sum(own * whole, axis=0, keepdims=True)
        part = merge_recv[:, :, t * LANES : (t + 1) * LANES].astype(F32)
        blended.append(jnp.sum(part * factor, axis=0))
    context = narrow(jnp.concatenate(blended, axis=1)).astype(BF16)

    def window(at, j):
        return pl.ds(pl.multiple_of(at * chunk + plan.first_of(j) * LANES, LANES), win)

    def cols_of(c):
        at = lax.rem(my_chunk + c, chunks)
        return pl.ds(pl.multiple_of(at * chunk, chunk), chunk)

    def scatter(phase, parts, product, source, target):
        own = slot(parts, grp, me)
        for c in [*range(1, chunks), 0]:
            cols = cols_of(c)
            made = product(cols)
            for g in range(parts):
                source[g, :, cols] = made[g * seqs : (g + 1) * seqs].astype(BF16)

            def send(g, peer, j, at):
                remote(
                    phase,
                    source.at[g if parts > 1 else 0, :, window(at, j)],
                    target.at[own],
                    recv_sem.at[phase, 0],
                    g,
                    peer,
                )

            reach(c, parts, send)
        target[own] = source[grp if parts > 1 else 0, :, window(my_chunk, my_place)]
        await_bytes(recv_sem.at[phase, 0], target, n * parts - 1)
        return jnp.sum(target[...].astype(F32), axis=0)

    def spread_rows(phase, parts, value, source, target):
        own = slot(parts, grp, me)
        source[...] = value
        for c in range(chunks):
            reach(
                c,
                parts,
                lambda g, peer, j, at: remote(
                    phase, source, target.at[own], recv_sem.at[phase, my_chunk], g, peer
                ),
            )
        target[own] = value

    def gathered(phase, parts, target, c):
        at = lax.rem(my_chunk + c, chunks)
        await_bytes(recv_sem.at[phase, at], target, parts * per - (c == 0))
        base = at * (parts * per)
        for g in range(parts):
            for t in range(tiles):
                whole = None
                for j in range(per):
                    k = t - plan.first[j]
                    if 0 <= k < plan.span:
                        piece = target[base + g * per + j, :, k * LANES : (k + 1) * LANES].astype(F32)
                        whole = piece if whole is None else whole + piece
                wide[g * seqs : (g + 1) * seqs, t * LANES : (t + 1) * LANES] = whole
        return wide[0 : parts * seqs, :]

    def normed(phase, parts, target, gain, matrices):
        sums = [None] * len(matrices)
        square = None
        for c in range(chunks):
            cols = cols_of(c)
            line = gathered(phase, parts, target, c)
            piece = (line * gain[:, cols]).astype(BF16)
            found = line * line
            square = found if square is None else square + found
            for i, matrix in enumerate(matrices):
                part = dot_rows(piece, matrix[:, cols])
                sums[i] = part if sums[i] is None else sums[i] + part
        mean = jnp.sum(square, axis=1, keepdims=True) * (1.0 / width)
        root = lax.rsqrt(mean + 1e-06)
        return [total * root for total in sums]

    total = scatter(
        SUM_A,
        1,
        lambda cols: jnp.dot(context, out_w[:, cols], preferred_element_type=F32),
        sum_a_send,
        sum_a_recv,
    )
    carried = jnp.where(mine, resting + total, 0.0).astype(BF16)
    spread_rows(ROW_A, share, carried, row_a_send, row_a_recv)
    loads[GAIN_A].wait()
    loads[GATE].wait()
    loads[UP].wait()
    gate, up = normed(ROW_A, share, row_a_recv, ffn_gain, (gate_w, up_w))
    activated = (gate / (1.0 + jnp.exp(-gate)) * up).astype(BF16)

    loads[DOWN].wait()
    total = scatter(
        SUM_B,
        share,
        lambda cols: jnp.dot(activated, down_w[:, cols], preferred_element_type=F32),
        sum_b_send,
        sum_b_recv,
    )
    leaving = jnp.where(mine, carried.astype(F32) + total, 0.0).astype(BF16)
    spread_rows(ROW_B, 1, leaving, row_b_send, row_b_recv)
    hidden_out[...] = narrow(leaving.astype(F32)).astype(BF16)
    loads[GAIN_B].wait()
    loads[QUERY].wait()
    (fresh,) = normed(ROW_B, 1, row_b_recv, query_gain, (query_w,))
    fresh = (fresh + query_bias[...][None, :]).astype(BF16).astype(F32)
    fresh = widen(fresh)

    device = lax.broadcasted_iota(jnp.int32, (n, win), 0)
    lines = jnp.zeros((n, win), F32)
    for s in range(seqs):
        lines = lines + jnp.where(device == home[s], fresh[s : s + 1], 0.0)
    for d in range(n):
        home_send[d] = lines[d : d + 1].astype(BF16)
    start(HOME, lambda peer: home_send.at[peer], home_recv)
    home_recv[me] = home_send[me]
    await_bytes(recv_sem.at[HOME, 0], home_recv, n - 1)
    for t in range(width // LANES):
        whole = None
        for j in range(per):
            k = t % tiles - plan.first[j]
            if 0 <= k < plan.span:
                d = (t // tiles) * per + j
                piece = home_recv[d, :, k * LANES : (k + 1) * LANES].astype(F32)
                whole = piece if whole is None else whole + piece
        next_out[:, t * LANES : (t + 1) * LANES] = whole.astype(BF16)

    await_bytes(send_sem.at[ASK], asked, n - 1)
    await_bytes(send_sem.at[MERGE], merge_recv, n - 1)
    await_bytes(send_sem.at[SUM_A], sum_a_recv, n - 1)
    await_bytes(send_sem.at[ROW_A], row_a_recv, n * share - 1)
    await_bytes(send_sem.at[SUM_B], sum_b_recv, n * share - 1)
    await_bytes(send_sem.at[ROW_B], row_b_recv, n - 1)
    await_bytes(send_sem.at[HOME], home_recv, n - 1)


def local(
    n,
    groups,
    queries,
    home_device,
    lengths,
    key_cache,
    value_cache,
    residual,
    out_weight,
    ffn_gain,
    gate_weight,
    up_weight,
    down_weight,
    query_gain,
    query_weight,
    query_bias,
):
    seqs, feat = residual.shape
    width = queries.shape[1]
    hidden = gate_weight.shape[1]
    share = groups if hidden % (16 * groups) == 0 else 1
    hidden //= share
    plan = Plan(n, width, 1280)
    win = plan.win
    vmem = pl.BlockSpec(memory_space=pltpu.VMEM)
    left = pl.BlockSpec(memory_space=pl.ANY)
    dma = pltpu.SemaphoreType.DMA

    def like(array):
        return pltpu.VMEM(array.shape, array.dtype)

    return pl.pallas_call(
        functools.partial(kernel, plan, share, groups),
        out_shape=(
            jax.ShapeDtypeStruct((seqs, feat), BF16),
            jax.ShapeDtypeStruct((1, width), BF16),
        ),
        in_specs=[left] * 2 + [vmem] + [left] * 11,
        out_specs=(vmem, vmem),
        scratch_shapes=[
            pltpu.SMEM(home_device.shape, home_device.dtype),
            pltpu.SMEM(lengths.shape, lengths.dtype),
            like(residual),
            pltpu.VMEM((1, width), F32),
            pltpu.VMEM((1, width), F32),
            like(key_cache),
            like(value_cache),
            like(out_weight),
            pltpu.VMEM((hidden, width), BF16),
            pltpu.VMEM((hidden, width), BF16),
            pltpu.VMEM((hidden, width), BF16),
            pltpu.VMEM((feat, width), BF16),
            pltpu.VMEM((n, 1, width), BF16),
            pltpu.VMEM((seqs, KVH, 8, HEAD), F32),
            pltpu.VMEM((seqs, width), F32),
            pltpu.VMEM((8, LANES), F32),
            pltpu.VMEM((n, seqs, win + LANES), BF16),
            pltpu.VMEM((n, seqs, win + LANES), BF16),
            pltpu.VMEM((1, seqs, width), BF16),
            pltpu.VMEM((n, seqs, win), BF16),
            pltpu.VMEM((seqs, win), BF16),
            pltpu.VMEM((n * share, seqs, win), BF16),
            pltpu.VMEM((share, seqs, width), BF16),
            pltpu.VMEM((n * share, seqs, win), BF16),
            pltpu.VMEM((seqs, win), BF16),
            pltpu.VMEM((n, seqs, win), BF16),
            pltpu.VMEM((n, 1, win), BF16),
            pltpu.VMEM((n, 1, win), BF16),
            pltpu.VMEM((len(plan.offsets), seqs, win), F32),
            pltpu.VMEM((seqs, win), F32),
            pltpu.VMEM((seqs * share, plan.chunk), F32),
            dma((13,)),
            dma((7,)),
            dma((7, plan.chunks)),
        ],
        compiler_params=pltpu.CompilerParams(
            collective_id=0, has_side_effects=True, vmem_limit_bytes=67043328
        ),
        name="decode_step",
    )(
        home_device,
        lengths,
        query_bias,
        queries,
        residual,
        ffn_gain[None, :],
        query_gain[None, :],
        key_cache,
        value_cache,
        out_weight,
        gate_weight.T,
        up_weight.T,
        down_weight,
        query_weight.T,
    )


def solution(mesh):
    placed = (
        P(("grp", "blk"), None),
        P("grp"),
        P("grp"),
        P("grp", "blk", None),
        P("grp", "blk", None),
        P("grp", "blk"),
        P("blk", None),
        P(),
        P(None, "blk"),
        P(None, "blk"),
        P("blk", None),
        P(),
        P(None, "blk"),
        P("blk"),
    )
    return jax.shard_map(
        functools.partial(local, mesh.shape["blk"], mesh.shape["grp"]),
        mesh=mesh,
        in_specs=placed,
        out_specs=(P("grp", "blk"), P(("grp", "blk"), None)),
        check_vma=False,
    )
```

```python
import functools
import math

import jax
import jax.numpy as jnp
from jax import lax
from jax.experimental import pallas as pl
from jax.experimental.pallas import tpu as pltpu
from jax.sharding import PartitionSpec as P

HQ = 40
KVH = 8
HEAD = 128
LANES = 128
GROUP = HQ // KVH
MESH = pl.DeviceIdType.MESH
F32 = jnp.float32
BF16 = jnp.bfloat16

ASK, MERGE, SUM_A, ROW_A, SUM_B, ROW_B, HOME = range(7)


class Plan:
    def __init__(self, n, width, wanted):
        self.n = n
        self.width = width
        self.feat = width // n
        unit = math.lcm(self.feat, LANES)
        self.chunk = unit
        while self.chunk * 2 <= wanted and width % (self.chunk * 2) == 0:
            self.chunk *= 2
        self.chunks = width // self.chunk
        self.per = self.chunk // self.feat
        self.tiles = self.chunk // LANES
        starts = [j * self.feat for j in range(self.per)]
        self.span = max(pl.cdiv(s % LANES + self.feat, LANES) for s in starts)
        self.clamped = any(s // LANES > self.tiles - self.span for s in starts)
        self.win = self.span * LANES
        self.first = [min(s // LANES, self.tiles - self.span) for s in starts]
        self.offsets = sorted({s - f * LANES for s, f in zip(starts, self.first)})

    def first_of(self, j):
        first = (j * self.feat) // LANES
        return jnp.minimum(first, self.tiles - self.span) if self.clamped else first


def dot_rows(left, right):
    return lax.dot_general(
        left, right, (((1,), (1,)), ((), ())), preferred_element_type=F32
    )


def kernel(
    plan,
    share,
    groups,
    home_hbm,
    length_hbm,
    bias_hbm,
    queries,
    residual_hbm,
    ffn_gain_hbm,
    query_gain_hbm,
    key_hbm,
    value_hbm,
    out_hbm,
    gate_hbm,
    up_hbm,
    down_hbm,
    query_hbm,
    hidden_out,
    next_out,
    home,
    length,
    residual,
    ffn_gain,
    query_gain,
    query_bias,
    keys,
    values,
    out_w,
    gate_w,
    up_w,
    down_w,
    query_w,
    line,
    lined,
    asked,
    heads,
    flat,
    stats,
    merge_send,
    merge_recv,
    sum_a_send,
    sum_a_recv,
    row_a_send,
    row_a_recv,
    sum_b_send,
    sum_b_recv,
    row_b_send,
    row_b_recv,
    home_send,
    home_recv,
    shifted,
    taken,
    wide,
    load_sem,
    send_sem,
    recv_sem,
):
    n, feat, width = plan.n, plan.feat, plan.width
    chunk, chunks, per, tiles = plan.chunk, plan.chunks, plan.per, plan.tiles
    win = plan.win
    me = lax.axis_index("blk")
    grp = lax.axis_index("grp")
    seqs = residual.shape[0]
    span = keys.shape[1]
    my_chunk = me // per
    my_place = lax.rem(me, per)
    hidden = gate_w.shape[0]
    shard = grp if share > 1 else 0
    half = pl.ds(pl.multiple_of(shard * hidden, 16), hidden)

    def load(src, dst, i):
        return pltpu.make_async_copy(src, dst, load_sem.at[i])

    loads = [
        load(src, dst, i)
        for i, (src, dst) in enumerate(
            (
                (queries, line),
                (home_hbm, home),
                (length_hbm, length),
                (key_hbm, keys),
                (value_hbm, values),
                (residual_hbm, residual),
                (out_hbm, out_w),
                (ffn_gain_hbm, ffn_gain),
                (gate_hbm.at[half], gate_w),
                (up_hbm.at[half], up_w),
                (down_hbm.at[half], down_w),
                (query_gain_hbm, query_gain),
                (query_hbm, query_w),
                (bias_hbm, query_bias),
            )
        )
    ]
    ASKED, HOMES, LENGTHS, KEYS, VALUES, REST, OUT, GAIN_A, GATE, UP, DOWN, GAIN_B, QUERY, BIAS = range(14)

    def each(low, high, action):
        def body(i, carry):
            action(i)
            return carry

        lax.fori_loop(low, high, body, 0, unroll=high - low <= 40)

    barrier = pltpu.get_barrier_semaphore()

    def greet(off):
        pl.semaphore_signal(
            barrier,
            inc=1,
            device_id={
                "grp": lax.rem(grp + off // n, share) if share > 1 else grp,
                "blk": lax.rem(me + off, n),
            },
            device_id_type=MESH,
        )

    loads[ASKED].start()
    each(1, n * share, greet)
    for one in loads[1:]:
        one.start()

    def remote(phase, source, target, sem, g, peer):
        pltpu.make_async_remote_copy(
            src_ref=source,
            dst_ref=target,
            send_sem=send_sem.at[phase],
            recv_sem=sem,
            device_id={"grp": g, "blk": peer},
            device_id_type=MESH,
        ).start()

    def start(phase, source, target):
        def send(off):
            peer = lax.rem(me + off, n)
            remote(phase, source(peer), target.at[me], recv_sem.at[phase, 0], grp, peer)

        each(1, n, send)

    def await_bytes(sem, target, count):
        part = target.at[pl.ds(0, count)]
        pltpu.make_async_copy(part, part, sem).wait()

    def slot(parts, g, peer):
        if parts == 1:
            return peer
        return (peer // per) * (parts * per) + g * per + lax.rem(peer, per)

    def reach(c, parts, action):
        at = lax.rem(my_chunk + c, chunks)

        def one(i):
            g = lax.rem(grp + i // per, parts) if parts > 1 else grp
            j = lax.rem(my_place + i, per)
            action(g, at * per + j, j, at)

        each(1 if c == 0 else 0, parts * per, one)

    heads[...] = jnp.zeros_like(heads)
    stats[...] = jnp.zeros_like(stats)
    shifted[...] = jnp.zeros_like(shifted)

    my_first = plan.first_of(my_place)
    offset = my_place * feat - my_first * LANES
    lane = lax.broadcasted_iota(jnp.int32, (seqs, win), 1)
    mine = (lane >= offset) & (lane < offset + feat)

    def narrow(value):
        taken[...] = value
        found = taken[:, plan.offsets[0] : plan.offsets[0] + feat]
        for o in plan.offsets[1:]:
            found = jnp.where(offset == o, taken[:, o : o + feat], found)
        return found

    def widen(value):
        for i, o in enumerate(plan.offsets):
            shifted[i, :, o : o + feat] = value
        found = shifted[0]
        for i, o in enumerate(plan.offsets[1:]):
            found = jnp.where(offset == o, shifted[i + 1], found)
        return found

    loads[ASKED].wait()
    whole_line = line[...].astype(F32)
    for h in range(HQ):
        lined[pl.ds(h, 1), :] = whole_line[:, h * HEAD : (h + 1) * HEAD]
    asked[me] = lined[...].astype(BF16)
    pl.semaphore_wait(barrier, n * share - 1)
    start(ASK, lambda peer: asked.at[me], asked)
    loads[HOMES].wait()
    loads[LENGTHS].wait()
    loads[REST].wait()
    resting = widen(residual[...].astype(F32))
    loads[KEYS].wait()
    loads[VALUES].wait()

    pad = 8
    rows = KVH * pad
    position = me * span + lax.broadcasted_iota(jnp.int32, (rows, span), 1)
    at_row = lax.broadcasted_iota(jnp.int32, (rows, LANES), 0)
    at_lane = lax.broadcasted_iota(jnp.int32, (rows, LANES), 1)
    row_head = (at_row // pad) * GROUP + lax.rem(at_row, pad)
    real = lax.rem(at_row, pad) < GROUP
    await_bytes(recv_sem.at[ASK, 0], asked, n - 1)
    for s in range(seqs):
        asking = asked[home[s]].astype(F32)
        for k in range(KVH):
            heads[s, k, 0:GROUP, :] = asking[k * GROUP : (k + 1) * GROUP]
        scores = jnp.concatenate(
            [
                dot_rows(heads[s, k].astype(BF16), keys[s, :, k * HEAD : (k + 1) * HEAD])
                for k in range(KVH)
            ],
            axis=0,
        ) * HEAD ** (-0.5)
        allowed = position < length[s]
        masked = jnp.where(allowed, scores, -1e30)
        peak = jnp.max(masked, axis=1, keepdims=True).astype(BF16).astype(F32)
        raised = jnp.where(allowed, jnp.exp(masked - peak), 0.0)
        total = jnp.sum(raised, axis=1, keepdims=True)
        high = total.astype(BF16).astype(F32)
        for k in range(KVH):
            mixed = jnp.dot(
                raised[k * pad : (k + 1) * pad].astype(BF16),
                values[s, :, k * HEAD : (k + 1) * HEAD],
                preferred_element_type=F32,
            )
            for g in range(GROUP):
                h = k * GROUP + g
                flat[pl.ds(s, 1), h * HEAD : (h + 1) * HEAD] = mixed[g : g + 1]
        spread = jnp.where(at_lane == row_head, peak, 0.0)
        spread = spread + jnp.where(at_lane == row_head + HQ, high, 0.0)
        spread = spread + jnp.where(at_lane == row_head + 2 * HQ, total - high, 0.0)
        stats[pl.ds(s, 1), :] = jnp.sum(jnp.where(real, spread, 0.0), axis=0, keepdims=True)

    noted = stats[...]
    for d in range(n):
        tile = (d // per) * tiles + plan.first[d % per]
        merge_send[d, :, 0:win] = flat[:, tile * LANES : tile * LANES + win].astype(BF16)
        rolled = pltpu.roll(noted, (LANES - tile) % LANES, 1) if tile else noted
        merge_send[d, :, win : win + LANES] = rolled[0:seqs].astype(BF16)
    start(MERGE, lambda peer: merge_send.at[peer], merge_recv)
    merge_recv[me] = merge_send[me]
    loads[OUT].wait()
    await_bytes(recv_sem.at[MERGE, 0], merge_recv, n - 1)

    stat = merge_recv[:, :, win : win + LANES].astype(F32)
    scale = jnp.exp(stat - jnp.max(stat, axis=0, keepdims=True))
    blended = []
    for t in range(plan.span):
        own = scale[:, :, t : t + 1]
        whole = stat[:, :, HQ + t : HQ + t + 1] + stat[:, :, 2 * HQ + t : 2 * HQ + t + 1]
        factor = own / jnp.sum(own * whole, axis=0, keepdims=True)
        part = merge_recv[:, :, t * LANES : (t + 1) * LANES].astype(F32)
        blended.append(jnp.sum(part * factor, axis=0))
    context = narrow(jnp.concatenate(blended, axis=1)).astype(BF16)

    def window(at, j):
        return pl.ds(pl.multiple_of(at * chunk + plan.first_of(j) * LANES, LANES), win)

    def cols_of(c):
        at = lax.rem(my_chunk + c, chunks)
        return pl.ds(pl.multiple_of(at * chunk, chunk), chunk)

    def scatter(phase, parts, product, source, target):
        own = slot(parts, grp, me)
        for c in [*range(1, chunks), 0]:
            cols = cols_of(c)
            made = product(cols)
            for g in range(parts):
                source[g, :, cols] = made[g * seqs : (g + 1) * seqs].astype(BF16)

            def send(g, peer, j, at):
                remote(
                    phase,
                    source.at[g if parts > 1 else 0, :, window(at, j)],
                    target.at[own],
                    recv_sem.at[phase, 0],
                    g,
                    peer,
                )

            reach(c, parts, send)
        target[own] = source[grp if parts > 1 else 0, :, window(my_chunk, my_place)]
        await_bytes(recv_sem.at[phase, 0], target, n * parts - 1)
        return jnp.sum(target[...].astype(F32), axis=0)

    def spread_rows(phase, parts, value, source, target):
        own = slot(parts, grp, me)
        source[...] = value
        for c in range(chunks):
            reach(
                c,
                parts,
                lambda g, peer, j, at: remote(
                    phase, source, target.at[own], recv_sem.at[phase, my_chunk], g, peer
                ),
            )
        target[own] = value

    def gathered(phase, parts, target, c):
        at = lax.rem(my_chunk + c, chunks)
        await_bytes(recv_sem.at[phase, at], target, parts * per - (c == 0))
        base = at * (parts * per)
        for g in range(parts):
            for t in range(tiles):
                whole = None
                for j in range(per):
                    k = t - plan.first[j]
                    if 0 <= k < plan.span:
                        piece = target[base + g * per + j, :, k * LANES : (k + 1) * LANES].astype(F32)
                        whole = piece if whole is None else whole + piece
                wide[g * seqs : (g + 1) * seqs, t * LANES : (t + 1) * LANES] = whole
        return wide[0 : parts * seqs, :]

    def normed(phase, parts, target, gain, matrices):
        sums = [None] * len(matrices)
        square = None
        for c in range(chunks):
            cols = cols_of(c)
            row = gathered(phase, parts, target, c)
            piece = (row * gain[:, cols]).astype(BF16)
            found = row * row
            square = found if square is None else square + found
            for i, matrix in enumerate(matrices):
                part = dot_rows(piece, matrix[:, cols])
                sums[i] = part if sums[i] is None else sums[i] + part
        mean = jnp.sum(square, axis=1, keepdims=True) * (1.0 / width)
        root = lax.rsqrt(mean + 1e-06)
        return [total * root for total in sums]

    total = scatter(
        SUM_A,
        1,
        lambda cols: jnp.dot(context, out_w[:, cols], preferred_element_type=F32),
        sum_a_send,
        sum_a_recv,
    )
    carried = jnp.where(mine, resting + total, 0.0).astype(BF16)
    spread_rows(ROW_A, share, carried, row_a_send, row_a_recv)
    loads[GAIN_A].wait()
    loads[GATE].wait()
    loads[UP].wait()
    gate, up = normed(ROW_A, share, row_a_recv, ffn_gain, (gate_w, up_w))
    activated = (gate / (1.0 + jnp.exp(-gate)) * up).astype(BF16)

    loads[DOWN].wait()
    total = scatter(
        SUM_B,
        share,
        lambda cols: jnp.dot(activated, down_w[:, cols], preferred_element_type=F32),
        sum_b_send,
        sum_b_recv,
    )
    leaving = jnp.where(mine, carried.astype(F32) + total, 0.0).astype(BF16)
    spread_rows(ROW_B, 1, leaving, row_b_send, row_b_recv)
    hidden_out[...] = narrow(leaving.astype(F32)).astype(BF16)
    loads[GAIN_B].wait()
    loads[QUERY].wait()
    loads[BIAS].wait()
    (fresh,) = normed(ROW_B, 1, row_b_recv, query_gain, (query_w,))
    fresh = (fresh + query_bias[...][None, :]).astype(BF16).astype(F32)
    fresh = widen(fresh)

    device = lax.broadcasted_iota(jnp.int32, (n, win), 0)
    lines = jnp.zeros((n, win), F32)
    for s in range(seqs):
        lines = lines + jnp.where(device == home[s], fresh[s : s + 1], 0.0)
    for d in range(n):
        home_send[d] = lines[d : d + 1].astype(BF16)
    start(HOME, lambda peer: home_send.at[peer], home_recv)
    home_recv[me] = home_send[me]
    await_bytes(recv_sem.at[HOME, 0], home_recv, n - 1)
    for t in range(width // LANES):
        whole = None
        for j in range(per):
            k = t % tiles - plan.first[j]
            if 0 <= k < plan.span:
                d = (t // tiles) * per + j
                piece = home_recv[d, :, k * LANES : (k + 1) * LANES].astype(F32)
                whole = piece if whole is None else whole + piece
        next_out[:, t * LANES : (t + 1) * LANES] = whole.astype(BF16)

    await_bytes(send_sem.at[ASK], asked, n - 1)
    await_bytes(send_sem.at[MERGE], merge_recv, n - 1)
    await_bytes(send_sem.at[SUM_A], sum_a_recv, n - 1)
    await_bytes(send_sem.at[ROW_A], row_a_recv, n * share - 1)
    await_bytes(send_sem.at[SUM_B], sum_b_recv, n * share - 1)
    await_bytes(send_sem.at[ROW_B], row_b_recv, n - 1)
    await_bytes(send_sem.at[HOME], home_recv, n - 1)


def local(
    n,
    groups,
    queries,
    home_device,
    lengths,
    key_cache,
    value_cache,
    residual,
    out_weight,
    ffn_gain,
    gate_weight,
    up_weight,
    down_weight,
    query_gain,
    query_weight,
    query_bias,
):
    seqs, feat = residual.shape
    width = queries.shape[1]
    hidden = gate_weight.shape[1]
    share = groups if hidden % (16 * groups) == 0 else 1
    hidden //= share
    plan = Plan(n, width, 1280)
    win = plan.win
    vmem = pl.BlockSpec(memory_space=pltpu.VMEM)
    left = pl.BlockSpec(memory_space=pl.ANY)
    dma = pltpu.SemaphoreType.DMA

    def like(array):
        return pltpu.VMEM(array.shape, array.dtype)

    leaving, asking = pl.pallas_call(
        functools.partial(kernel, plan, share, groups),
        out_shape=(
            jax.ShapeDtypeStruct((seqs, feat), BF16),
            jax.ShapeDtypeStruct((1, width), BF16),
        ),
        in_specs=[left] * 14,
        out_specs=(vmem, vmem),
        scratch_shapes=[
            pltpu.SMEM(home_device.shape, home_device.dtype),
            pltpu.SMEM(lengths.shape, lengths.dtype),
            like(residual),
            pltpu.VMEM((1, width), F32),
            pltpu.VMEM((1, width), F32),
            pltpu.VMEM((feat,), F32),
            like(key_cache),
            like(value_cache),
            like(out_weight),
            pltpu.VMEM((hidden, width), BF16),
            pltpu.VMEM((hidden, width), BF16),
            pltpu.VMEM((hidden, width), BF16),
            pltpu.VMEM((feat, width), BF16),
            pltpu.VMEM((1, width), BF16),
            pltpu.VMEM((HQ, HEAD), F32),
            pltpu.VMEM((n, HQ, HEAD), BF16),
            pltpu.VMEM((seqs, KVH, 8, HEAD), F32),
            pltpu.VMEM((seqs, width), F32),
            pltpu.VMEM((8, LANES), F32),
            pltpu.VMEM((n, seqs, win + LANES), BF16),
            pltpu.VMEM((n, seqs, win + LANES), BF16),
            pltpu.VMEM((1, seqs, width), BF16),
            pltpu.VMEM((n, seqs, win), BF16),
            pltpu.VMEM((seqs, win), BF16),
            pltpu.VMEM((n * share, seqs, win), BF16),
            pltpu.VMEM((share, seqs, width), BF16),
            pltpu.VMEM((n * share, seqs, win), BF16),
            pltpu.VMEM((seqs, win), BF16),
            pltpu.VMEM((n, seqs, win), BF16),
            pltpu.VMEM((n, 1, win), BF16),
            pltpu.VMEM((n, 1, win), BF16),
            pltpu.VMEM((len(plan.offsets), seqs, win), F32),
            pltpu.VMEM((seqs, win), F32),
            pltpu.VMEM((seqs * share, plan.chunk), F32),
            dma((14,)),
            dma((7,)),
            dma((7, plan.chunks)),
        ],
        compiler_params=pltpu.CompilerParams(
            collective_id=0, has_side_effects=True, vmem_limit_bytes=67043328
        ),
        name="decode_step",
    )(
        home_device,
        lengths,
        query_bias,
        queries,
        residual,
        ffn_gain[None, :],
        query_gain[None, :],
        key_cache,
        value_cache,
        out_weight,
        gate_weight.T,
        up_weight.T,
        down_weight,
        query_weight.T,
    )

    def hand_on(source_a, source_b, target_a, target_b, sem):
        copies = [
            pltpu.make_async_copy(source_a, target_a, sem.at[0]),
            pltpu.make_async_copy(source_b, target_b, sem.at[1]),
        ]
        for copy in copies:
            copy.start()
        for copy in copies:
            copy.wait()

    return pl.pallas_call(
        hand_on,
        out_shape=(
            jax.ShapeDtypeStruct((seqs, feat), BF16),
            jax.ShapeDtypeStruct((1, width), BF16),
        ),
        in_specs=[left] * 2,
        out_specs=(left, left),
        scratch_shapes=[dma((2,))],
        name="hand_on",
    )(leaving, asking)


def solution(mesh):
    placed = (
        P(("grp", "blk"), None),
        P("grp"),
        P("grp"),
        P("grp", "blk", None),
        P("grp", "blk", None),
        P("grp", "blk"),
        P("blk", None),
        P(),
        P(None, "blk"),
        P(None, "blk"),
        P("blk", None),
        P(),
        P(None, "blk"),
        P("blk"),
    )
    return jax.shard_map(
        functools.partial(local, mesh.shape["blk"], mesh.shape["grp"]),
        mesh=mesh,
        in_specs=placed,
        out_specs=(P("grp", "blk"), P(("grp", "blk"), None)),
        check_vma=False,
    )
```

```python
import functools
import math

import jax
import jax.numpy as jnp
from jax import lax
from jax.experimental import pallas as pl
from jax.experimental.pallas import tpu as pltpu
from jax.sharding import PartitionSpec as P

HQ = 40
KVH = 8
HEAD = 128
LANES = 128
GROUP = HQ // KVH
MESH = pl.DeviceIdType.MESH
F32 = jnp.float32
BF16 = jnp.bfloat16

ASK, MERGE, SUM_A, ROW_A, SUM_B, ROW_B, HOME = range(7)


class Plan:
    def __init__(self, n, width, wanted):
        self.n = n
        self.width = width
        self.feat = width // n
        unit = math.lcm(self.feat, LANES)
        self.chunk = unit
        while self.chunk * 2 <= wanted and width % (self.chunk * 2) == 0:
            self.chunk *= 2
        self.chunks = width // self.chunk
        self.per = self.chunk // self.feat
        self.tiles = self.chunk // LANES
        starts = [j * self.feat for j in range(self.per)]
        self.span = max(pl.cdiv(s % LANES + self.feat, LANES) for s in starts)
        self.clamped = any(s // LANES > self.tiles - self.span for s in starts)
        self.win = self.span * LANES
        self.first = [min(s // LANES, self.tiles - self.span) for s in starts]
        self.offsets = sorted({s - f * LANES for s, f in zip(starts, self.first)})

    def first_of(self, j):
        first = (j * self.feat) // LANES
        return jnp.minimum(first, self.tiles - self.span) if self.clamped else first


def dot_rows(left, right):
    return lax.dot_general(
        left, right, (((1,), (1,)), ((), ())), preferred_element_type=F32
    )


def kernel(
    plan,
    share,
    groups,
    home_hbm,
    length_hbm,
    bias_hbm,
    queries,
    residual_hbm,
    ffn_gain_hbm,
    query_gain_hbm,
    key_hbm,
    value_hbm,
    out_hbm,
    gate_hbm,
    up_hbm,
    down_hbm,
    query_hbm,
    hidden_out,
    next_out,
    home,
    length,
    residual,
    ffn_gain,
    query_gain,
    query_bias,
    keys,
    values,
    out_w,
    gate_w,
    up_w,
    down_w,
    query_w,
    gate_t,
    up_t,
    query_t,
    line,
    lined,
    asked,
    heads,
    flat,
    stats,
    merge_send,
    merge_recv,
    sum_a_send,
    sum_a_recv,
    row_a_send,
    row_a_recv,
    sum_b_send,
    sum_b_recv,
    row_b_send,
    row_b_recv,
    home_send,
    home_recv,
    shifted,
    taken,
    wide,
    load_sem,
    send_sem,
    recv_sem,
):
    n, feat, width = plan.n, plan.feat, plan.width
    chunk, chunks, per, tiles = plan.chunk, plan.chunks, plan.per, plan.tiles
    win = plan.win
    me = lax.axis_index("blk")
    grp = lax.axis_index("grp")
    seqs = residual.shape[0]
    span = keys.shape[1]
    my_chunk = me // per
    my_place = lax.rem(me, per)
    hidden = gate_w.shape[0]
    shard = grp if share > 1 else 0
    half = pl.ds(pl.multiple_of(shard * hidden, 16), hidden)

    def load(src, dst, i):
        return pltpu.make_async_copy(src, dst, load_sem.at[i])

    loads = [
        load(src, dst, i)
        for i, (src, dst) in enumerate(
            (
                (queries, line),
                (home_hbm, home),
                (length_hbm, length),
                (key_hbm, keys),
                (value_hbm, values),
                (residual_hbm, residual),
                (gate_hbm.at[half], gate_w),
                (up_hbm.at[half], up_w),
                (out_hbm, out_w),
                (ffn_gain_hbm, ffn_gain),
                (down_hbm.at[half], down_w),
                (query_gain_hbm, query_gain),
                (query_hbm, query_w),
                (bias_hbm, query_bias),
            )
        )
    ]
    ASKED, HOMES, LENGTHS, KEYS, VALUES, REST, GATE, UP, OUT, GAIN_A, DOWN, GAIN_B, QUERY, BIAS = range(14)

    def each(low, high, action, unroll=True):
        def body(i, carry):
            action(i)
            return carry

        lax.fori_loop(low, high, body, 0, unroll=unroll)

    barrier = pltpu.get_barrier_semaphore()

    def greet(off):
        pl.semaphore_signal(
            barrier,
            inc=1,
            device_id={
                "grp": lax.rem(grp + off // n, share) if share > 1 else grp,
                "blk": lax.rem(me + off, n),
            },
            device_id_type=MESH,
        )

    loads[ASKED].start()
    each(1, n * share, greet)
    for one in loads[1:]:
        one.start()

    def remote(phase, source, target, sem, g, peer):
        pltpu.make_async_remote_copy(
            src_ref=source,
            dst_ref=target,
            send_sem=send_sem.at[phase],
            recv_sem=sem,
            device_id={"grp": g, "blk": peer},
            device_id_type=MESH,
        ).start()

    def start(phase, source, target):
        def send(off):
            peer = lax.rem(me + off, n)
            remote(phase, source(peer), target.at[me], recv_sem.at[phase, 0], grp, peer)

        each(1, n, send)

    def await_bytes(sem, target, count):
        part = target.at[pl.ds(0, count)]
        pltpu.make_async_copy(part, part, sem).wait()

    def slot(parts, g, peer):
        if parts == 1:
            return peer
        return (peer // per) * (parts * per) + g * per + lax.rem(peer, per)

    def reach(c, parts, action):
        at = lax.rem(my_chunk + c, chunks)

        def one(i):
            g = lax.rem(grp + i // per, parts) if parts > 1 else grp
            j = lax.rem(my_place + i, per)
            action(g, at * per + j, j, at)

        each(1 if c == 0 else 0, parts * per, one)

    def turn(source, target, block):
        def one(i):
            at = pl.ds(pl.multiple_of(i * block, block), block)
            target[at, :] = source[:, at].T

        each(0, width // block, one, 1)

    heads[...] = jnp.zeros_like(heads)
    stats[...] = jnp.zeros_like(stats)
    shifted[...] = jnp.zeros_like(shifted)

    my_first = plan.first_of(my_place)
    offset = my_place * feat - my_first * LANES
    lane = lax.broadcasted_iota(jnp.int32, (seqs, win), 1)
    mine = (lane >= offset) & (lane < offset + feat)

    def narrow(value):
        taken[...] = value
        found = taken[:, plan.offsets[0] : plan.offsets[0] + feat]
        for o in plan.offsets[1:]:
            found = jnp.where(offset == o, taken[:, o : o + feat], found)
        return found

    def widen(value):
        for i, o in enumerate(plan.offsets):
            shifted[i, :, o : o + feat] = value
        found = shifted[0]
        for i, o in enumerate(plan.offsets[1:]):
            found = jnp.where(offset == o, shifted[i + 1], found)
        return found

    loads[ASKED].wait()
    whole_line = line[...].astype(F32)
    for h in range(HQ):
        lined[pl.ds(h, 1), :] = whole_line[:, h * HEAD : (h + 1) * HEAD]
    asked[me] = lined[...].astype(BF16)
    pl.semaphore_wait(barrier, n * share - 1)
    start(ASK, lambda peer: asked.at[me], asked)
    loads[HOMES].wait()
    loads[LENGTHS].wait()
    loads[REST].wait()
    resting = widen(residual[...].astype(F32))
    loads[KEYS].wait()
    loads[VALUES].wait()

    pad = 8
    rows = KVH * pad
    position = me * span + lax.broadcasted_iota(jnp.int32, (rows, span), 1)
    at_row = lax.broadcasted_iota(jnp.int32, (rows, LANES), 0)
    at_lane = lax.broadcasted_iota(jnp.int32, (rows, LANES), 1)
    row_head = (at_row // pad) * GROUP + lax.rem(at_row, pad)
    real = lax.rem(at_row, pad) < GROUP
    loads[GATE].wait()
    turn(gate_w, gate_t, 256)
    await_bytes(recv_sem.at[ASK, 0], asked, n - 1)
    for s in range(seqs):
        asking = asked[home[s]].astype(F32)
        for k in range(KVH):
            heads[s, k, 0:GROUP, :] = asking[k * GROUP : (k + 1) * GROUP]
        scores = jnp.concatenate(
            [
                dot_rows(heads[s, k].astype(BF16), keys[s, :, k * HEAD : (k + 1) * HEAD])
                for k in range(KVH)
            ],
            axis=0,
        ) * HEAD ** (-0.5)
        allowed = position < length[s]
        masked = jnp.where(allowed, scores, -1e30)
        peak = jnp.max(masked, axis=1, keepdims=True).astype(BF16).astype(F32)
        raised = jnp.where(allowed, jnp.exp(masked - peak), 0.0)
        total = jnp.sum(raised, axis=1, keepdims=True)
        high = total.astype(BF16).astype(F32)
        for k in range(KVH):
            mixed = jnp.dot(
                raised[k * pad : (k + 1) * pad].astype(BF16),
                values[s, :, k * HEAD : (k + 1) * HEAD],
                preferred_element_type=F32,
            )
            for g in range(GROUP):
                h = k * GROUP + g
                flat[pl.ds(s, 1), h * HEAD : (h + 1) * HEAD] = mixed[g : g + 1]
        spread = jnp.where(at_lane == row_head, peak, 0.0)
        spread = spread + jnp.where(at_lane == row_head + HQ, high, 0.0)
        spread = spread + jnp.where(at_lane == row_head + 2 * HQ, total - high, 0.0)
        stats[pl.ds(s, 1), :] = jnp.sum(jnp.where(real, spread, 0.0), axis=0, keepdims=True)

    noted = stats[...]
    for d in range(n):
        tile = (d // per) * tiles + plan.first[d % per]
        merge_send[d, :, 0:win] = flat[:, tile * LANES : tile * LANES + win].astype(BF16)
        rolled = pltpu.roll(noted, (LANES - tile) % LANES, 1) if tile else noted
        merge_send[d, :, win : win + LANES] = rolled[0:seqs].astype(BF16)
    start(MERGE, lambda peer: merge_send.at[peer], merge_recv)
    merge_recv[me] = merge_send[me]
    loads[UP].wait()
    turn(up_w, up_t, 256)
    loads[OUT].wait()
    await_bytes(recv_sem.at[MERGE, 0], merge_recv, n - 1)

    stat = merge_recv[:, :, win : win + LANES].astype(F32)
    scale = jnp.exp(stat - jnp.max(stat, axis=0, keepdims=True))
    blended = []
    for t in range(plan.span):
        own = scale[:, :, t : t + 1]
        whole = stat[:, :, HQ + t : HQ + t + 1] + stat[:, :, 2 * HQ + t : 2 * HQ + t + 1]
        factor = own / jnp.sum(own * whole, axis=0, keepdims=True)
        part = merge_recv[:, :, t * LANES : (t + 1) * LANES].astype(F32)
        blended.append(jnp.sum(part * factor, axis=0))
    context = narrow(jnp.concatenate(blended, axis=1)).astype(BF16)

    def window(at, j):
        return pl.ds(pl.multiple_of(at * chunk + plan.first_of(j) * LANES, LANES), win)

    def cols_of(c):
        at = lax.rem(my_chunk + c, chunks)
        return pl.ds(pl.multiple_of(at * chunk, chunk), chunk)

    def scatter(phase, parts, product, source, target, meanwhile):
        own = slot(parts, grp, me)
        for c in [*range(1, chunks), 0]:
            cols = cols_of(c)
            made = product(cols)
            for g in range(parts):
                source[g, :, cols] = made[g * seqs : (g + 1) * seqs].astype(BF16)

            def send(g, peer, j, at):
                remote(
                    phase,
                    source.at[g if parts > 1 else 0, :, window(at, j)],
                    target.at[own],
                    recv_sem.at[phase, 0],
                    g,
                    peer,
                )

            reach(c, parts, send)
        target[own] = source[grp if parts > 1 else 0, :, window(my_chunk, my_place)]
        meanwhile()
        await_bytes(recv_sem.at[phase, 0], target, n * parts - 1)
        return jnp.sum(target[...].astype(F32), axis=0)

    def spread_rows(phase, parts, value, source, target):
        own = slot(parts, grp, me)
        source[...] = value
        for c in range(chunks):
            reach(
                c,
                parts,
                lambda g, peer, j, at: remote(
                    phase, source, target.at[own], recv_sem.at[phase, my_chunk], g, peer
                ),
            )
        target[own] = value

    def gathered(phase, parts, target, c):
        at = lax.rem(my_chunk + c, chunks)
        await_bytes(recv_sem.at[phase, at], target, parts * per - (c == 0))
        base = at * (parts * per)
        for g in range(parts):
            for t in range(tiles):
                whole = None
                for j in range(per):
                    k = t - plan.first[j]
                    if 0 <= k < plan.span:
                        piece = target[base + g * per + j, :, k * LANES : (k + 1) * LANES].astype(F32)
                        whole = piece if whole is None else whole + piece
                wide[g * seqs : (g + 1) * seqs, t * LANES : (t + 1) * LANES] = whole
        return wide[0 : parts * seqs, :]

    def normed(phase, parts, target, gain, matrices):
        sums = [None] * len(matrices)
        square = None
        for c in range(chunks):
            cols = cols_of(c)
            row = gathered(phase, parts, target, c)
            piece = (row * gain[:, cols]).astype(BF16)
            found = row * row
            square = found if square is None else square + found
            for i, matrix in enumerate(matrices):
                part = jnp.dot(piece, matrix[cols, :], preferred_element_type=F32)
                sums[i] = part if sums[i] is None else sums[i] + part
        mean = jnp.sum(square, axis=1, keepdims=True) * (1.0 / width)
        root = lax.rsqrt(mean + 1e-06)
        return [total * root for total in sums]

    def turn_query():
        loads[QUERY].wait()
        turn(query_w, query_t, 512)

    total = scatter(
        SUM_A,
        1,
        lambda cols: jnp.dot(context, out_w[:, cols], preferred_element_type=F32),
        sum_a_send,
        sum_a_recv,
        turn_query,
    )
    carried = jnp.where(mine, resting + total, 0.0).astype(BF16)
    spread_rows(ROW_A, share, carried, row_a_send, row_a_recv)
    loads[GAIN_A].wait()
    gate, up = normed(ROW_A, share, row_a_recv, ffn_gain, (gate_t, up_t))
    activated = (gate / (1.0 + jnp.exp(-gate)) * up).astype(BF16)

    loads[DOWN].wait()
    total = scatter(
        SUM_B,
        share,
        lambda cols: jnp.dot(activated, down_w[:, cols], preferred_element_type=F32),
        sum_b_send,
        sum_b_recv,
        lambda: None,
    )
    leaving = jnp.where(mine, carried.astype(F32) + total, 0.0).astype(BF16)
    spread_rows(ROW_B, 1, leaving, row_b_send, row_b_recv)
    hidden_out[...] = narrow(leaving.astype(F32)).astype(BF16)
    loads[GAIN_B].wait()
    loads[BIAS].wait()
    (fresh,) = normed(ROW_B, 1, row_b_recv, query_gain, (query_t,))
    fresh = (fresh + query_bias[...][None, :]).astype(BF16).astype(F32)
    fresh = widen(fresh)

    device = lax.broadcasted_iota(jnp.int32, (n, win), 0)
    lines = jnp.zeros((n, win), F32)
    for s in range(seqs):
        lines = lines + jnp.where(device == home[s], fresh[s : s + 1], 0.0)
    for d in range(n):
        home_send[d] = lines[d : d + 1].astype(BF16)
    start(HOME, lambda peer: home_send.at[peer], home_recv)
    home_recv[me] = home_send[me]
    await_bytes(recv_sem.at[HOME, 0], home_recv, n - 1)
    for t in range(width // LANES):
        whole = None
        for j in range(per):
            k = t % tiles - plan.first[j]
            if 0 <= k < plan.span:
                d = (t // tiles) * per + j
                piece = home_recv[d, :, k * LANES : (k + 1) * LANES].astype(F32)
                whole = piece if whole is None else whole + piece
        next_out[:, t * LANES : (t + 1) * LANES] = whole.astype(BF16)

    await_bytes(send_sem.at[ASK], asked, n - 1)
    await_bytes(send_sem.at[MERGE], merge_recv, n - 1)
    await_bytes(send_sem.at[SUM_A], sum_a_recv, n - 1)
    await_bytes(send_sem.at[ROW_A], row_a_recv, n * share - 1)
    await_bytes(send_sem.at[SUM_B], sum_b_recv, n * share - 1)
    await_bytes(send_sem.at[ROW_B], row_b_recv, n - 1)
    await_bytes(send_sem.at[HOME], home_recv, n - 1)


def local(
    n,
    groups,
    queries,
    home_device,
    lengths,
    key_cache,
    value_cache,
    residual,
    out_weight,
    ffn_gain,
    gate_weight,
    up_weight,
    down_weight,
    query_gain,
    query_weight,
    query_bias,
):
    seqs, feat = residual.shape
    width = queries.shape[1]
    hidden = gate_weight.shape[1]
    share = groups if hidden % (16 * groups) == 0 else 1
    hidden //= share
    plan = Plan(n, width, 1280)
    win = plan.win
    vmem = pl.BlockSpec(memory_space=pltpu.VMEM)
    left = pl.BlockSpec(memory_space=pl.ANY)
    dma = pltpu.SemaphoreType.DMA

    def like(array):
        return pltpu.VMEM(array.shape, array.dtype)

    leaving, asking = pl.pallas_call(
        functools.partial(kernel, plan, share, groups),
        out_shape=(
            jax.ShapeDtypeStruct((seqs, feat), BF16),
            jax.ShapeDtypeStruct((1, width), BF16),
        ),
        in_specs=[left] * 14,
        out_specs=(vmem, vmem),
        scratch_shapes=[
            pltpu.SMEM(home_device.shape, home_device.dtype),
            pltpu.SMEM(lengths.shape, lengths.dtype),
            like(residual),
            pltpu.VMEM((1, width), F32),
            pltpu.VMEM((1, width), F32),
            pltpu.VMEM((feat,), F32),
            like(key_cache),
            like(value_cache),
            like(out_weight),
            pltpu.VMEM((hidden, width), BF16),
            pltpu.VMEM((hidden, width), BF16),
            pltpu.VMEM((hidden, width), BF16),
            pltpu.VMEM((feat, width), BF16),
            pltpu.VMEM((width, hidden), BF16),
            pltpu.VMEM((width, hidden), BF16),
            pltpu.VMEM((width, feat), BF16),
            pltpu.VMEM((1, width), BF16),
            pltpu.VMEM((HQ, HEAD), F32),
            pltpu.VMEM((n, HQ, HEAD), BF16),
            pltpu.VMEM((seqs, KVH, 8, HEAD), F32),
            pltpu.VMEM((seqs, width), F32),
            pltpu.VMEM((8, LANES), F32),
            pltpu.VMEM((n, seqs, win + LANES), BF16),
            pltpu.VMEM((n, seqs, win + LANES), BF16),
            pltpu.VMEM((1, seqs, width), BF16),
            pltpu.VMEM((n, seqs, win), BF16),
            pltpu.VMEM((seqs, win), BF16),
            pltpu.VMEM((n * share, seqs, win), BF16),
            pltpu.VMEM((share, seqs, width), BF16),
            pltpu.VMEM((n * share, seqs, win), BF16),
            pltpu.VMEM((seqs, win), BF16),
            pltpu.VMEM((n, seqs, win), BF16),
            pltpu.VMEM((n, 1, win), BF16),
            pltpu.VMEM((n, 1, win), BF16),
            pltpu.VMEM((len(plan.offsets), seqs, win), F32),
            pltpu.VMEM((seqs, win), F32),
            pltpu.VMEM((seqs * share, plan.chunk), F32),
            dma((14,)),
            dma((7,)),
            dma((7, plan.chunks)),
        ],
        compiler_params=pltpu.CompilerParams(
            collective_id=0, has_side_effects=True, vmem_limit_bytes=67043328
        ),
        name="decode_step",
    )(
        home_device,
        lengths,
        query_bias,
        queries,
        residual,
        ffn_gain[None, :],
        query_gain[None, :],
        key_cache,
        value_cache,
        out_weight,
        gate_weight.T,
        up_weight.T,
        down_weight,
        query_weight.T,
    )

    def hand_on(source_a, source_b, target_a, target_b, sem):
        copies = [
            pltpu.make_async_copy(source_a, target_a, sem.at[0]),
            pltpu.make_async_copy(source_b, target_b, sem.at[1]),
        ]
        for copy in copies:
            copy.start()
        for copy in copies:
            copy.wait()

    return pl.pallas_call(
        hand_on,
        out_shape=(
            jax.ShapeDtypeStruct((seqs, feat), BF16),
            jax.ShapeDtypeStruct((1, width), BF16),
        ),
        in_specs=[left] * 2,
        out_specs=(left, left),
        scratch_shapes=[dma((2,))],
        name="hand_on",
    )(leaving, asking)


def solution(mesh):
    placed = (
        P(("grp", "blk"), None),
        P("grp"),
        P("grp"),
        P("grp", "blk", None),
        P("grp", "blk", None),
        P("grp", "blk"),
        P("blk", None),
        P(),
        P(None, "blk"),
        P(None, "blk"),
        P("blk", None),
        P(),
        P(None, "blk"),
        P("blk"),
    )
    return jax.shard_map(
        functools.partial(local, mesh.shape["blk"], mesh.shape["grp"]),
        mesh=mesh,
        in_specs=placed,
        out_specs=(P("grp", "blk"), P(("grp", "blk"), None)),
        check_vma=False,
    )
```

```python
import functools
import math

import jax
import jax.numpy as jnp
from jax import lax
from jax.experimental import pallas as pl
from jax.experimental.pallas import tpu as pltpu
from jax.sharding import PartitionSpec as P

HQ = 40
KVH = 8
HEAD = 128
LANES = 128
GROUP = HQ // KVH
MESH = pl.DeviceIdType.MESH
F32 = jnp.float32
BF16 = jnp.bfloat16

ASK, MERGE, SUM_A, ROW_A, SUM_B, ROW_B, HOME = range(7)


class Plan:
    def __init__(self, n, width, wanted):
        self.n = n
        self.width = width
        self.feat = width // n
        unit = math.lcm(self.feat, LANES)
        self.chunk = unit
        while self.chunk * 2 <= wanted and width % (self.chunk * 2) == 0:
            self.chunk *= 2
        self.chunks = width // self.chunk
        self.per = self.chunk // self.feat
        self.tiles = self.chunk // LANES
        starts = [j * self.feat for j in range(self.per)]
        self.span = max(pl.cdiv(s % LANES + self.feat, LANES) for s in starts)
        self.clamped = any(s // LANES > self.tiles - self.span for s in starts)
        self.win = self.span * LANES
        self.first = [min(s // LANES, self.tiles - self.span) for s in starts]
        self.offsets = sorted({s - f * LANES for s, f in zip(starts, self.first)})

    def first_of(self, j):
        first = (j * self.feat) // LANES
        return jnp.minimum(first, self.tiles - self.span) if self.clamped else first


def dot_rows(left, right):
    return lax.dot_general(
        left, right, (((1,), (1,)), ((), ())), preferred_element_type=F32
    )


def kernel(
    plan,
    share,
    groups,
    home_hbm,
    length_hbm,
    bias_hbm,
    queries,
    residual_hbm,
    ffn_gain_hbm,
    query_gain_hbm,
    key_hbm,
    value_hbm,
    out_hbm,
    gate_hbm,
    up_hbm,
    down_hbm,
    query_hbm,
    hidden_out,
    next_out,
    home,
    length,
    residual,
    ffn_gain,
    query_gain,
    query_bias,
    keys,
    values,
    out_w,
    gate_w,
    up_w,
    down_w,
    query_w,
    gate_t,
    up_t,
    query_t,
    line,
    lined,
    asked,
    heads,
    flat,
    stats,
    merge_send,
    merge_recv,
    sum_a_send,
    sum_a_recv,
    row_a_send,
    row_a_recv,
    sum_b_send,
    sum_b_recv,
    row_b_send,
    row_b_recv,
    home_send,
    home_recv,
    shifted,
    taken,
    wide,
    load_sem,
    send_sem,
    recv_sem,
):
    n, feat, width = plan.n, plan.feat, plan.width
    chunk, chunks, per, tiles = plan.chunk, plan.chunks, plan.per, plan.tiles
    win = plan.win
    me = lax.axis_index("blk")
    grp = lax.axis_index("grp")
    seqs = residual.shape[0]
    span = keys.shape[1]
    my_chunk = me // per
    my_place = lax.rem(me, per)
    hidden = gate_w.shape[0]
    shard = grp if share > 1 else 0
    half = pl.ds(pl.multiple_of(shard * hidden, 16), hidden)

    def load(src, dst, i):
        return pltpu.make_async_copy(src, dst, load_sem.at[i])

    loads = [
        load(src, dst, i)
        for i, (src, dst) in enumerate(
            (
                (queries, line),
                (home_hbm, home),
                (length_hbm, length),
                (key_hbm, keys),
                (value_hbm, values),
                (residual_hbm, residual),
                (gate_hbm.at[half], gate_w),
                (up_hbm.at[half], up_w),
                (out_hbm, out_w),
                (ffn_gain_hbm, ffn_gain),
                (down_hbm.at[half], down_w),
                (query_gain_hbm, query_gain),
                (query_hbm, query_w),
                (bias_hbm, query_bias),
            )
        )
    ]
    ASKED, HOMES, LENGTHS, KEYS, VALUES, REST, GATE, UP, OUT, GAIN_A, DOWN, GAIN_B, QUERY, BIAS = range(14)

    def each(low, high, action, unroll=True):
        def body(i, carry):
            action(i)
            return carry

        lax.fori_loop(low, high, body, 0, unroll=unroll)

    barrier = pltpu.get_barrier_semaphore()

    def greet(off):
        pl.semaphore_signal(
            barrier,
            inc=1,
            device_id={
                "grp": lax.rem(grp + off // n, share) if share > 1 else grp,
                "blk": lax.rem(me + off, n),
            },
            device_id_type=MESH,
        )

    each(1, n * share, greet)
    loads[ASKED].start()
    for one in loads[1:]:
        one.start()

    def remote(phase, source, target, sem, g, peer):
        pltpu.make_async_remote_copy(
            src_ref=source,
            dst_ref=target,
            send_sem=send_sem.at[phase],
            recv_sem=sem,
            device_id={"grp": g, "blk": peer},
            device_id_type=MESH,
        ).start()

    def start(phase, source, target):
        for c in reversed(range(chunks)):
            reach(
                c,
                1,
                lambda g, peer, j, at: remote(
                    phase, source(peer), target.at[me], recv_sem.at[phase, 0], g, peer
                ),
            )

    def await_bytes(sem, target, count):
        part = target.at[pl.ds(0, count)]
        pltpu.make_async_copy(part, part, sem).wait()

    def slot(parts, g, peer):
        if parts == 1:
            return peer
        return (peer // per) * (parts * per) + g * per + lax.rem(peer, per)

    def partner(c):
        if chunks & (chunks - 1):
            return lax.rem(my_chunk + c, chunks)
        at, bit = my_chunk, 1
        while bit < chunks:
            if c & bit:
                at = at + bit - 2 * bit * lax.rem(my_chunk // bit, 2)
            bit *= 2
        return at

    def reach(c, parts, action):
        at = partner(c)

        def one(i):
            g = lax.rem(grp + i // per, parts) if parts > 1 else grp
            j = lax.rem(my_place + i, per)
            action(g, at * per + j, j, at)

        each(1 if c == 0 else 0, parts * per, one)

    def turn(source, target, block):
        def one(i):
            at = pl.ds(pl.multiple_of(i * block, block), block)
            target[at, :] = source[:, at].T

        each(0, width // block, one, 1)

    heads[...] = jnp.zeros_like(heads)
    stats[...] = jnp.zeros_like(stats)
    shifted[...] = jnp.zeros_like(shifted)

    my_first = plan.first_of(my_place)
    offset = my_place * feat - my_first * LANES
    lane = lax.broadcasted_iota(jnp.int32, (seqs, win), 1)
    mine = (lane >= offset) & (lane < offset + feat)

    def narrow(value):
        taken[...] = value
        found = taken[:, plan.offsets[0] : plan.offsets[0] + feat]
        for o in plan.offsets[1:]:
            found = jnp.where(offset == o, taken[:, o : o + feat], found)
        return found

    def widen(value):
        for i, o in enumerate(plan.offsets):
            shifted[i, :, o : o + feat] = value
        found = shifted[0]
        for i, o in enumerate(plan.offsets[1:]):
            found = jnp.where(offset == o, shifted[i + 1], found)
        return found

    loads[ASKED].wait()
    whole_line = line[...].astype(F32)
    for h in range(HQ):
        lined[pl.ds(h, 1), :] = whole_line[:, h * HEAD : (h + 1) * HEAD]
    asked[me] = lined[...].astype(BF16)
    pl.semaphore_wait(barrier, n * share - 1)
    start(ASK, lambda peer: asked.at[me], asked)
    loads[HOMES].wait()
    loads[LENGTHS].wait()
    loads[REST].wait()
    resting = widen(residual[...].astype(F32))
    loads[KEYS].wait()
    loads[VALUES].wait()

    pad = 8
    rows = KVH * pad
    position = me * span + lax.broadcasted_iota(jnp.int32, (rows, span), 1)
    at_row = lax.broadcasted_iota(jnp.int32, (rows, LANES), 0)
    at_lane = lax.broadcasted_iota(jnp.int32, (rows, LANES), 1)
    row_head = (at_row // pad) * GROUP + lax.rem(at_row, pad)
    real = lax.rem(at_row, pad) < GROUP
    loads[GATE].wait()
    turn(gate_w, gate_t, 512)
    await_bytes(recv_sem.at[ASK, 0], asked, n - 1)
    for s in range(seqs):
        asking = asked[home[s]].astype(F32)
        for k in range(KVH):
            heads[s, k, 0:GROUP, :] = asking[k * GROUP : (k + 1) * GROUP]
        scores = jnp.concatenate(
            [
                dot_rows(heads[s, k].astype(BF16), keys[s, :, k * HEAD : (k + 1) * HEAD])
                for k in range(KVH)
            ],
            axis=0,
        ) * HEAD ** (-0.5)
        allowed = position < length[s]
        masked = jnp.where(allowed, scores, -1e30)
        peak = jnp.max(masked, axis=1, keepdims=True).astype(BF16).astype(F32)
        raised = jnp.where(allowed, jnp.exp(masked - peak), 0.0)
        total = jnp.sum(raised, axis=1, keepdims=True)
        high = total.astype(BF16).astype(F32)
        for k in range(KVH):
            mixed = jnp.dot(
                raised[k * pad : (k + 1) * pad].astype(BF16),
                values[s, :, k * HEAD : (k + 1) * HEAD],
                preferred_element_type=F32,
            )
            for g in range(GROUP):
                h = k * GROUP + g
                flat[pl.ds(s, 1), h * HEAD : (h + 1) * HEAD] = mixed[g : g + 1]
        spread = jnp.where(at_lane == row_head, peak, 0.0)
        spread = spread + jnp.where(at_lane == row_head + HQ, high, 0.0)
        spread = spread + jnp.where(at_lane == row_head + 2 * HQ, total - high, 0.0)
        stats[pl.ds(s, 1), :] = jnp.sum(jnp.where(real, spread, 0.0), axis=0, keepdims=True)

    noted = stats[...]
    for d in range(n):
        tile = (d // per) * tiles + plan.first[d % per]
        merge_send[d, :, 0:win] = flat[:, tile * LANES : tile * LANES + win].astype(BF16)
        rolled = pltpu.roll(noted, (LANES - tile) % LANES, 1) if tile else noted
        merge_send[d, :, win : win + LANES] = rolled[0:seqs].astype(BF16)
    start(MERGE, lambda peer: merge_send.at[peer], merge_recv)
    merge_recv[me] = merge_send[me]
    loads[UP].wait()
    turn(up_w, up_t, 512)
    loads[OUT].wait()
    await_bytes(recv_sem.at[MERGE, 0], merge_recv, n - 1)

    stat = merge_recv[:, :, win : win + LANES].astype(F32)
    scale = jnp.exp(stat - jnp.max(stat, axis=0, keepdims=True))
    blended = []
    for t in range(plan.span):
        own = scale[:, :, t : t + 1]
        whole = stat[:, :, HQ + t : HQ + t + 1] + stat[:, :, 2 * HQ + t : 2 * HQ + t + 1]
        factor = own / jnp.sum(own * whole, axis=0, keepdims=True)
        part = merge_recv[:, :, t * LANES : (t + 1) * LANES].astype(F32)
        blended.append(jnp.sum(part * factor, axis=0))
    context = narrow(jnp.concatenate(blended, axis=1)).astype(BF16)

    def window(at, j):
        return pl.ds(pl.multiple_of(at * chunk + plan.first_of(j) * LANES, LANES), win)

    def cols_of(c):
        at = partner(c)
        return pl.ds(pl.multiple_of(at * chunk, chunk), chunk)

    def scatter(phase, parts, product, source, target, meanwhile):
        own = slot(parts, grp, me)
        for c in reversed(range(chunks)):
            cols = cols_of(c)
            made = product(cols)
            for g in range(parts):
                source[g, :, cols] = made[g * seqs : (g + 1) * seqs].astype(BF16)

            def send(g, peer, j, at):
                remote(
                    phase,
                    source.at[g if parts > 1 else 0, :, window(at, j)],
                    target.at[own],
                    recv_sem.at[phase, 0],
                    g,
                    peer,
                )

            reach(c, parts, send)
        target[own] = source[grp if parts > 1 else 0, :, window(my_chunk, my_place)]
        meanwhile()
        await_bytes(recv_sem.at[phase, 0], target, n * parts - 1)
        return jnp.sum(target[...].astype(F32), axis=0)

    def spread_rows(phase, parts, value, source, target):
        own = slot(parts, grp, me)
        source[...] = value
        for c in [0, *reversed(range(1, chunks))]:
            reach(
                c,
                parts,
                lambda g, peer, j, at: remote(
                    phase, source, target.at[own], recv_sem.at[phase, my_chunk], g, peer
                ),
            )
        target[own] = value

    def gathered(phase, parts, target, c):
        at = partner(c)
        await_bytes(recv_sem.at[phase, at], target, parts * per - (c == 0))
        base = at * (parts * per)
        for g in range(parts):
            for t in range(tiles):
                whole = None
                for j in range(per):
                    k = t - plan.first[j]
                    if 0 <= k < plan.span:
                        piece = target[base + g * per + j, :, k * LANES : (k + 1) * LANES].astype(F32)
                        whole = piece if whole is None else whole + piece
                wide[g * seqs : (g + 1) * seqs, t * LANES : (t + 1) * LANES] = whole
        return wide[0 : parts * seqs, :]

    def normed(phase, parts, target, gain, matrices):
        sums = [None] * len(matrices)
        square = None
        for c in range(chunks):
            cols = cols_of(c)
            row = gathered(phase, parts, target, c)
            piece = (row * gain[:, cols]).astype(BF16)
            found = row * row
            square = found if square is None else square + found
            for i, matrix in enumerate(matrices):
                part = jnp.dot(piece, matrix[cols, :], preferred_element_type=F32)
                sums[i] = part if sums[i] is None else sums[i] + part
        mean = jnp.sum(square, axis=1, keepdims=True) * (1.0 / width)
        root = lax.rsqrt(mean + 1e-06)
        return [total * root for total in sums]

    def turn_query():
        loads[QUERY].wait()
        turn(query_w, query_t, 512)

    total = scatter(
        SUM_A,
        1,
        lambda cols: jnp.dot(context, out_w[:, cols], preferred_element_type=F32),
        sum_a_send,
        sum_a_recv,
        turn_query,
    )
    carried = jnp.where(mine, resting + total, 0.0).astype(BF16)
    spread_rows(ROW_A, share, carried, row_a_send, row_a_recv)
    loads[GAIN_A].wait()
    gate, up = normed(ROW_A, share, row_a_recv, ffn_gain, (gate_t, up_t))
    activated = (gate / (1.0 + jnp.exp(-gate)) * up).astype(BF16)

    loads[DOWN].wait()
    total = scatter(
        SUM_B,
        share,
        lambda cols: jnp.dot(activated, down_w[:, cols], preferred_element_type=F32),
        sum_b_send,
        sum_b_recv,
        lambda: None,
    )
    leaving = jnp.where(mine, carried.astype(F32) + total, 0.0).astype(BF16)
    spread_rows(ROW_B, 1, leaving, row_b_send, row_b_recv)
    hidden_out[...] = narrow(leaving.astype(F32)).astype(BF16)
    loads[GAIN_B].wait()
    loads[BIAS].wait()
    (fresh,) = normed(ROW_B, 1, row_b_recv, query_gain, (query_t,))
    fresh = (fresh + query_bias[...][None, :]).astype(BF16).astype(F32)
    fresh = widen(fresh)

    device = lax.broadcasted_iota(jnp.int32, (n, win), 0)
    lines = jnp.zeros((n, win), F32)
    for s in range(seqs):
        lines = lines + jnp.where(device == home[s], fresh[s : s + 1], 0.0)
    for d in range(n):
        home_send[d] = lines[d : d + 1].astype(BF16)
    start(HOME, lambda peer: home_send.at[peer], home_recv)
    home_recv[me] = home_send[me]
    await_bytes(recv_sem.at[HOME, 0], home_recv, n - 1)
    for t in range(width // LANES):
        whole = None
        for j in range(per):
            k = t % tiles - plan.first[j]
            if 0 <= k < plan.span:
                d = (t // tiles) * per + j
                piece = home_recv[d, :, k * LANES : (k + 1) * LANES].astype(F32)
                whole = piece if whole is None else whole + piece
        next_out[:, t * LANES : (t + 1) * LANES] = whole.astype(BF16)

    await_bytes(send_sem.at[ASK], asked, n - 1)
    await_bytes(send_sem.at[MERGE], merge_recv, n - 1)
    await_bytes(send_sem.at[SUM_A], sum_a_recv, n - 1)
    await_bytes(send_sem.at[ROW_A], row_a_recv, n * share - 1)
    await_bytes(send_sem.at[SUM_B], sum_b_recv, n * share - 1)
    await_bytes(send_sem.at[ROW_B], row_b_recv, n - 1)
    await_bytes(send_sem.at[HOME], home_recv, n - 1)


def local(
    n,
    groups,
    queries,
    home_device,
    lengths,
    key_cache,
    value_cache,
    residual,
    out_weight,
    ffn_gain,
    gate_weight,
    up_weight,
    down_weight,
    query_gain,
    query_weight,
    query_bias,
):
    seqs, feat = residual.shape
    width = queries.shape[1]
    hidden = gate_weight.shape[1]
    share = groups if hidden % (16 * groups) == 0 else 1
    hidden //= share
    plan = Plan(n, width, 1280)
    win = plan.win
    vmem = pl.BlockSpec(memory_space=pltpu.VMEM)
    left = pl.BlockSpec(memory_space=pl.ANY)
    dma = pltpu.SemaphoreType.DMA

    def like(array):
        return pltpu.VMEM(array.shape, array.dtype)

    leaving, asking = pl.pallas_call(
        functools.partial(kernel, plan, share, groups),
        out_shape=(
            jax.ShapeDtypeStruct((seqs, feat), BF16),
            jax.ShapeDtypeStruct((1, width), BF16),
        ),
        in_specs=[left] * 14,
        out_specs=(vmem, vmem),
        scratch_shapes=[
            pltpu.SMEM(home_device.shape, home_device.dtype),
            pltpu.SMEM(lengths.shape, lengths.dtype),
            like(residual),
            pltpu.VMEM((1, width), F32),
            pltpu.VMEM((1, width), F32),
            pltpu.VMEM((feat,), F32),
            like(key_cache),
            like(value_cache),
            like(out_weight),
            pltpu.VMEM((hidden, width), BF16),
            pltpu.VMEM((hidden, width), BF16),
            pltpu.VMEM((hidden, width), BF16),
            pltpu.VMEM((feat, width), BF16),
            pltpu.VMEM((width, hidden), BF16),
            pltpu.VMEM((width, hidden), BF16),
            pltpu.VMEM((width, feat), BF16),
            pltpu.VMEM((1, width), BF16),
            pltpu.VMEM((HQ, HEAD), F32),
            pltpu.VMEM((n, HQ, HEAD), BF16),
            pltpu.VMEM((seqs, KVH, 8, HEAD), F32),
            pltpu.VMEM((seqs, width), F32),
            pltpu.VMEM((8, LANES), F32),
            pltpu.VMEM((n, seqs, win + LANES), BF16),
            pltpu.VMEM((n, seqs, win + LANES), BF16),
            pltpu.VMEM((1, seqs, width), BF16),
            pltpu.VMEM((n, seqs, win), BF16),
            pltpu.VMEM((seqs, win), BF16),
            pltpu.VMEM((n * share, seqs, win), BF16),
            pltpu.VMEM((share, seqs, width), BF16),
            pltpu.VMEM((n * share, seqs, win), BF16),
            pltpu.VMEM((seqs, win), BF16),
            pltpu.VMEM((n, seqs, win), BF16),
            pltpu.VMEM((n, 1, win), BF16),
            pltpu.VMEM((n, 1, win), BF16),
            pltpu.VMEM((len(plan.offsets), seqs, win), F32),
            pltpu.VMEM((seqs, win), F32),
            pltpu.VMEM((seqs * share, plan.chunk), F32),
            dma((14,)),
            dma((7,)),
            dma((7, plan.chunks)),
        ],
        compiler_params=pltpu.CompilerParams(
            collective_id=0, has_side_effects=True, vmem_limit_bytes=67043328
        ),
        name="decode_step",
    )(
        home_device,
        lengths,
        query_bias,
        queries,
        residual,
        ffn_gain[None, :],
        query_gain[None, :],
        key_cache,
        value_cache,
        out_weight,
        gate_weight.T,
        up_weight.T,
        down_weight,
        query_weight.T,
    )

    def hand_on(source_a, source_b, target_a, target_b, held_a, held_b, sem):
        copies = [
            pltpu.make_async_copy(source_b, held_b, sem.at[0]),
            pltpu.make_async_copy(source_a, held_a, sem.at[1]),
            pltpu.make_async_copy(held_b, target_b, sem.at[2]),
            pltpu.make_async_copy(held_a, target_a, sem.at[3]),
        ]
        copies[0].start()
        copies[1].start()
        copies[0].wait()
        copies[2].start()
        copies[1].wait()
        copies[3].start()
        copies[2].wait()
        copies[3].wait()

    return pl.pallas_call(
        hand_on,
        out_shape=(
            jax.ShapeDtypeStruct((seqs, feat), BF16),
            jax.ShapeDtypeStruct((1, width), BF16),
        ),
        in_specs=[left] * 2,
        out_specs=(left, left),
        scratch_shapes=[
            pltpu.VMEM((seqs, feat), BF16),
            pltpu.VMEM((1, width), BF16),
            dma((4,)),
        ],
        name="hand_on",
    )(leaving, asking)


def solution(mesh):
    placed = (
        P(("grp", "blk"), None),
        P("grp"),
        P("grp"),
        P("grp", "blk", None),
        P("grp", "blk", None),
        P("grp", "blk"),
        P("blk", None),
        P(),
        P(None, "blk"),
        P(None, "blk"),
        P("blk", None),
        P(),
        P(None, "blk"),
        P("blk"),
    )
    return jax.shard_map(
        functools.partial(local, mesh.shape["blk"], mesh.shape["grp"]),
        mesh=mesh,
        in_specs=placed,
        out_specs=(P("grp", "blk"), P(("grp", "blk"), None)),
        check_vma=False,
    )
```

```python
import functools
import math

import jax
import jax.numpy as jnp
from jax import lax
from jax.experimental import pallas as pl
from jax.experimental.pallas import tpu as pltpu
from jax.sharding import PartitionSpec as P

HQ = 40
KVH = 8
HEAD = 128
LANES = 128
GROUP = HQ // KVH
MESH = pl.DeviceIdType.MESH
F32 = jnp.float32
BF16 = jnp.bfloat16

ASK, MERGE, SUM_A, ROW_A, SUM_B, ROW_B, HOME = range(7)


class Plan:
    def __init__(self, n, width, wanted):
        self.n = n
        self.width = width
        self.feat = width // n
        unit = math.lcm(self.feat, LANES)
        self.chunk = unit
        while self.chunk * 2 <= wanted and width % (self.chunk * 2) == 0:
            self.chunk *= 2
        self.chunks = width // self.chunk
        self.per = self.chunk // self.feat
        self.tiles = self.chunk // LANES
        starts = [j * self.feat for j in range(self.per)]
        self.span = max(pl.cdiv(s % LANES + self.feat, LANES) for s in starts)
        self.clamped = any(s // LANES > self.tiles - self.span for s in starts)
        self.win = self.span * LANES
        self.first = [min(s // LANES, self.tiles - self.span) for s in starts]
        self.offsets = sorted({s - f * LANES for s, f in zip(starts, self.first)})

    def first_of(self, j):
        first = (j * self.feat) // LANES
        return jnp.minimum(first, self.tiles - self.span) if self.clamped else first


def dot_rows(left, right):
    return lax.dot_general(
        left, right, (((1,), (1,)), ((), ())), preferred_element_type=F32
    )


def kernel(
    plan,
    share,
    groups,
    home_hbm,
    length_hbm,
    bias_hbm,
    queries,
    residual_hbm,
    ffn_gain_hbm,
    query_gain_hbm,
    key_hbm,
    value_hbm,
    out_hbm,
    gate_hbm,
    up_hbm,
    down_hbm,
    query_hbm,
    hidden_out,
    next_out,
    home,
    length,
    residual,
    ffn_gain,
    query_gain,
    query_bias,
    keys,
    values,
    out_w,
    gate_w,
    up_w,
    down_w,
    query_w,
    gate_t,
    up_t,
    query_t,
    line,
    lined,
    asked,
    heads,
    flat,
    stats,
    merge_send,
    merge_recv,
    sum_a_send,
    sum_a_recv,
    row_a_send,
    row_a_recv,
    sum_b_send,
    sum_b_recv,
    row_b_send,
    row_b_recv,
    home_send,
    home_recv,
    shifted,
    taken,
    wide,
    load_sem,
    send_sem,
    recv_sem,
):
    n, feat, width = plan.n, plan.feat, plan.width
    chunk, chunks, per, tiles = plan.chunk, plan.chunks, plan.per, plan.tiles
    win = plan.win
    me = lax.axis_index("blk")
    grp = lax.axis_index("grp")
    seqs = residual.shape[0]
    span = keys.shape[1]
    my_chunk = me // per
    my_place = lax.rem(me, per)
    hidden = gate_w.shape[0]
    shard = grp if share > 1 else 0
    half = pl.ds(pl.multiple_of(shard * hidden, 16), hidden)

    def load(src, dst, i):
        return pltpu.make_async_copy(src, dst, load_sem.at[i])

    loads = [
        load(src, dst, i)
        for i, (src, dst) in enumerate(
            (
                (queries, line),
                (home_hbm, home),
                (length_hbm, length),
                (key_hbm, keys),
                (value_hbm, values),
                (residual_hbm, residual),
                (gate_hbm.at[half], gate_w),
                (up_hbm.at[half], up_w),
                (out_hbm, out_w),
                (ffn_gain_hbm, ffn_gain),
                (down_hbm.at[half], down_w),
                (query_gain_hbm, query_gain),
                (query_hbm, query_w),
                (bias_hbm, query_bias),
            )
        )
    ]
    ASKED, HOMES, LENGTHS, KEYS, VALUES, REST, GATE, UP, OUT, GAIN_A, DOWN, GAIN_B, QUERY, BIAS = range(14)

    def each(low, high, action, unroll=True):
        def body(i, carry):
            action(i)
            return carry

        lax.fori_loop(low, high, body, 0, unroll=unroll)

    def remote(phase, source, target, sem, g, peer):
        pltpu.make_async_remote_copy(
            src_ref=source,
            dst_ref=target,
            send_sem=send_sem.at[phase],
            recv_sem=sem,
            device_id={"grp": g, "blk": peer},
            device_id_type=MESH,
        ).start()

    def start(phase, source, target):
        for c in reversed(range(chunks)):
            reach(
                c,
                1,
                lambda g, peer, j, at: remote(
                    phase, source(peer), target.at[me], recv_sem.at[phase, 0], g, peer
                ),
            )

    def await_bytes(sem, target, count):
        part = target.at[pl.ds(0, count)]
        pltpu.make_async_copy(part, part, sem).wait()

    def slot(parts, g, peer):
        if parts == 1:
            return peer
        return (peer // per) * (parts * per) + g * per + lax.rem(peer, per)

    def partner(c):
        if chunks & (chunks - 1):
            return lax.rem(my_chunk + c, chunks)
        at, bit = my_chunk, 1
        while bit < chunks:
            if c & bit:
                at = at + bit - 2 * bit * lax.rem(my_chunk // bit, 2)
            bit *= 2
        return at

    def reach(c, parts, action):
        at = partner(c)

        def one(i):
            g = lax.rem(grp + parts - 1 - i // per, parts) if parts > 1 else grp
            j = lax.rem(my_place + i, per)
            action(g, at * per + j, j, at)

        skip = (parts - 1) * per
        if c:
            each(0, parts * per, one)
        else:
            if parts > 1:
                each(0, skip, one)
            each(skip + 1, parts * per, one)

    barrier = pltpu.get_barrier_semaphore()

    def greet(g, peer, j, at):
        pl.semaphore_signal(
            barrier, inc=1, device_id={"grp": g, "blk": peer}, device_id_type=MESH
        )

    for c in reversed(range(chunks)):
        reach(c, share, greet)
    for one in loads:
        one.start()

    def turn(source, target, block):
        def one(i):
            at = pl.ds(pl.multiple_of(i * block, block), block)
            target[at, :] = source[:, at].T

        each(0, width // block, one, 1)

    heads[...] = jnp.zeros_like(heads)
    stats[...] = jnp.zeros_like(stats)
    shifted[...] = jnp.zeros_like(shifted)

    my_first = plan.first_of(my_place)
    offset = my_place * feat - my_first * LANES
    lane = lax.broadcasted_iota(jnp.int32, (seqs, win), 1)
    mine = (lane >= offset) & (lane < offset + feat)

    def narrow(value):
        taken[...] = value
        found = taken[:, plan.offsets[0] : plan.offsets[0] + feat]
        for o in plan.offsets[1:]:
            found = jnp.where(offset == o, taken[:, o : o + feat], found)
        return found

    def widen(value):
        for i, o in enumerate(plan.offsets):
            shifted[i, :, o : o + feat] = value
        found = shifted[0]
        for i, o in enumerate(plan.offsets[1:]):
            found = jnp.where(offset == o, shifted[i + 1], found)
        return found

    loads[ASKED].wait()
    whole_line = line[...].astype(F32)
    for h in range(HQ):
        lined[pl.ds(h, 1), :] = whole_line[:, h * HEAD : (h + 1) * HEAD]
    asked[me] = lined[...].astype(BF16)
    pl.semaphore_wait(barrier, n * share - 1)
    start(ASK, lambda peer: asked.at[me], asked)
    loads[HOMES].wait()
    loads[LENGTHS].wait()
    loads[REST].wait()
    resting = widen(residual[...].astype(F32))
    loads[KEYS].wait()
    loads[VALUES].wait()

    pad = 8
    rows = KVH * pad
    position = me * span + lax.broadcasted_iota(jnp.int32, (rows, span), 1)
    at_row = lax.broadcasted_iota(jnp.int32, (rows, LANES), 0)
    at_lane = lax.broadcasted_iota(jnp.int32, (rows, LANES), 1)
    row_head = (at_row // pad) * GROUP + lax.rem(at_row, pad)
    real = lax.rem(at_row, pad) < GROUP
    loads[GATE].wait()
    turn(gate_w, gate_t, 512)
    await_bytes(recv_sem.at[ASK, 0], asked, n - 1)
    for s in range(seqs):
        asking = asked[home[s]].astype(F32)
        for k in range(KVH):
            heads[s, k, 0:GROUP, :] = asking[k * GROUP : (k + 1) * GROUP]
    scores = [
        jnp.concatenate(
            [
                dot_rows(heads[s, k].astype(BF16), keys[s, :, k * HEAD : (k + 1) * HEAD])
                for k in range(KVH)
            ],
            axis=0,
        ) * HEAD ** (-0.5)
        for s in range(seqs)
    ]
    allowed = [position < length[s] for s in range(seqs)]
    masked = [jnp.where(allowed[s], scores[s], -1e30) for s in range(seqs)]
    peaks = [
        jnp.max(masked[s], axis=1, keepdims=True).astype(BF16).astype(F32) for s in range(seqs)
    ]
    raised = [
        jnp.where(allowed[s], jnp.exp(masked[s] - peaks[s]), 0.0) for s in range(seqs)
    ]
    for s in range(seqs):
        for k in range(KVH):
            mixed = jnp.dot(
                raised[s][k * pad : (k + 1) * pad].astype(BF16),
                values[s, :, k * HEAD : (k + 1) * HEAD],
                preferred_element_type=F32,
            )
            for g in range(GROUP):
                h = k * GROUP + g
                flat[pl.ds(s, 1), h * HEAD : (h + 1) * HEAD] = mixed[g : g + 1]
    for s in range(seqs):
        total = jnp.sum(raised[s], axis=1, keepdims=True)
        high = total.astype(BF16).astype(F32)
        spread = jnp.where(at_lane == row_head, peaks[s], 0.0)
        spread = spread + jnp.where(at_lane == row_head + HQ, high, 0.0)
        spread = spread + jnp.where(at_lane == row_head + 2 * HQ, total - high, 0.0)
        stats[pl.ds(s, 1), :] = jnp.sum(jnp.where(real, spread, 0.0), axis=0, keepdims=True)

    noted = stats[...]
    for d in range(n):
        tile = (d // per) * tiles + plan.first[d % per]
        merge_send[d, :, 0:win] = flat[:, tile * LANES : tile * LANES + win].astype(BF16)
        rolled = pltpu.roll(noted, (LANES - tile) % LANES, 1) if tile else noted
        merge_send[d, :, win : win + LANES] = rolled[0:seqs].astype(BF16)
    start(MERGE, lambda peer: merge_send.at[peer], merge_recv)
    merge_recv[me] = merge_send[me]
    loads[UP].wait()
    turn(up_w, up_t, 512)
    loads[OUT].wait()
    await_bytes(recv_sem.at[MERGE, 0], merge_recv, n - 1)

    stat = merge_recv[:, :, win : win + LANES].astype(F32)
    scale = jnp.exp(stat - jnp.max(stat, axis=0, keepdims=True))
    flat_stat = stat.reshape(n * seqs, LANES)
    whole = pltpu.roll(flat_stat, LANES - HQ, 1) + pltpu.roll(flat_stat, LANES - 2 * HQ, 1)
    whole = whole.reshape(n, seqs, LANES)
    factors = scale / jnp.sum(scale * whole, axis=0, keepdims=True)
    blended = []
    for t in range(plan.span):
        part = merge_recv[:, :, t * LANES : (t + 1) * LANES].astype(F32)
        blended.append(jnp.sum(part * factors[:, :, t : t + 1], axis=0))
    context = narrow(jnp.concatenate(blended, axis=1)).astype(BF16)

    def window(at, j):
        return pl.ds(pl.multiple_of(at * chunk + plan.first_of(j) * LANES, LANES), win)

    def cols_of(c):
        at = partner(c)
        return pl.ds(pl.multiple_of(at * chunk, chunk), chunk)

    def scatter(phase, parts, product, source, target, meanwhile):
        own = slot(parts, grp, me)
        for c in reversed(range(chunks)):
            cols = cols_of(c)
            made = product(cols)
            for g in range(parts):
                source[g, :, cols] = made[g * seqs : (g + 1) * seqs].astype(BF16)

            def send(g, peer, j, at):
                remote(
                    phase,
                    source.at[g if parts > 1 else 0, :, window(at, j)],
                    target.at[own],
                    recv_sem.at[phase, 0],
                    g,
                    peer,
                )

            reach(c, parts, send)
        target[own] = source[grp if parts > 1 else 0, :, window(my_chunk, my_place)]
        meanwhile()
        await_bytes(recv_sem.at[phase, 0], target, n * parts - 1)
        return jnp.sum(target[...].astype(F32), axis=0)

    def spread_rows(phase, parts, value, source, target):
        own = slot(parts, grp, me)
        source[...] = value
        for c in [0, *reversed(range(1, chunks))]:
            reach(
                c,
                parts,
                lambda g, peer, j, at: remote(
                    phase, source, target.at[own], recv_sem.at[phase, my_chunk], g, peer
                ),
            )
        target[own] = value

    def gathered(phase, parts, target, c):
        at = partner(c)
        await_bytes(recv_sem.at[phase, at], target, parts * per - (c == 0))
        base = at * (parts * per)
        for g in range(parts):
            for t in range(tiles):
                whole = None
                for j in range(per):
                    k = t - plan.first[j]
                    if 0 <= k < plan.span:
                        piece = target[base + g * per + j, :, k * LANES : (k + 1) * LANES].astype(F32)
                        whole = piece if whole is None else whole + piece
                wide[g * seqs : (g + 1) * seqs, t * LANES : (t + 1) * LANES] = whole
        return wide[0 : parts * seqs, :]

    def normed(phase, parts, target, gain, matrices):
        sums = [None] * len(matrices)
        square = None
        for c in range(chunks):
            cols = cols_of(c)
            row = gathered(phase, parts, target, c)
            piece = (row * gain[:, cols]).astype(BF16)
            found = row * row
            square = found if square is None else square + found
            for i, matrix in enumerate(matrices):
                part = jnp.dot(piece, matrix[cols, :], preferred_element_type=F32)
                sums[i] = part if sums[i] is None else sums[i] + part
        mean = jnp.sum(square, axis=1, keepdims=True) * (1.0 / width)
        root = lax.rsqrt(mean + 1e-06)
        return [total * root for total in sums]

    def turn_query():
        loads[QUERY].wait()
        turn(query_w, query_t, 512)

    total = scatter(
        SUM_A,
        1,
        lambda cols: jnp.dot(context, out_w[:, cols], preferred_element_type=F32),
        sum_a_send,
        sum_a_recv,
        turn_query,
    )
    carried = jnp.where(mine, resting + total, 0.0).astype(BF16)
    spread_rows(ROW_A, share, carried, row_a_send, row_a_recv)
    loads[GAIN_A].wait()
    gate, up = normed(ROW_A, share, row_a_recv, ffn_gain, (gate_t, up_t))
    activated = (gate / (1.0 + jnp.exp(-gate)) * up).astype(BF16)

    loads[DOWN].wait()
    total = scatter(
        SUM_B,
        share,
        lambda cols: jnp.dot(activated, down_w[:, cols], preferred_element_type=F32),
        sum_b_send,
        sum_b_recv,
        lambda: None,
    )
    leaving = jnp.where(mine, carried.astype(F32) + total, 0.0).astype(BF16)
    spread_rows(ROW_B, 1, leaving, row_b_send, row_b_recv)
    hidden_out[...] = narrow(leaving.astype(F32)).astype(BF16)
    loads[GAIN_B].wait()
    loads[BIAS].wait()
    (fresh,) = normed(ROW_B, 1, row_b_recv, query_gain, (query_t,))
    fresh = (fresh + query_bias[...][None, :]).astype(BF16).astype(F32)
    fresh = widen(fresh)

    device = lax.broadcasted_iota(jnp.int32, (n, win), 0)
    lines = jnp.zeros((n, win), F32)
    for s in range(seqs):
        lines = lines + jnp.where(device == home[s], fresh[s : s + 1], 0.0)
    for d in range(n):
        home_send[d] = lines[d : d + 1].astype(BF16)
    start(HOME, lambda peer: home_send.at[peer], home_recv)
    home_recv[me] = home_send[me]
    await_bytes(recv_sem.at[HOME, 0], home_recv, n - 1)
    for t in range(width // LANES):
        whole = None
        for j in range(per):
            k = t % tiles - plan.first[j]
            if 0 <= k < plan.span:
                d = (t // tiles) * per + j
                piece = home_recv[d, :, k * LANES : (k + 1) * LANES].astype(F32)
                whole = piece if whole is None else whole + piece
        next_out[:, t * LANES : (t + 1) * LANES] = whole.astype(BF16)

    await_bytes(send_sem.at[ASK], asked, n - 1)
    await_bytes(send_sem.at[MERGE], merge_recv, n - 1)
    await_bytes(send_sem.at[SUM_A], sum_a_recv, n - 1)
    await_bytes(send_sem.at[ROW_A], row_a_recv, n * share - 1)
    await_bytes(send_sem.at[SUM_B], sum_b_recv, n * share - 1)
    await_bytes(send_sem.at[ROW_B], row_b_recv, n - 1)
    await_bytes(send_sem.at[HOME], home_recv, n - 1)


def local(
    n,
    groups,
    queries,
    home_device,
    lengths,
    key_cache,
    value_cache,
    residual,
    out_weight,
    ffn_gain,
    gate_weight,
    up_weight,
    down_weight,
    query_gain,
    query_weight,
    query_bias,
):
    seqs, feat = residual.shape
    width = queries.shape[1]
    hidden = gate_weight.shape[1]
    share = groups if hidden % (16 * groups) == 0 else 1
    hidden //= share
    plan = Plan(n, width, 1280)
    win = plan.win
    vmem = pl.BlockSpec(memory_space=pltpu.VMEM)
    left = pl.BlockSpec(memory_space=pl.ANY)
    dma = pltpu.SemaphoreType.DMA

    def like(array):
        return pltpu.VMEM(array.shape, array.dtype)

    leaving, asking = pl.pallas_call(
        functools.partial(kernel, plan, share, groups),
        out_shape=(
            jax.ShapeDtypeStruct((seqs, feat), BF16),
            jax.ShapeDtypeStruct((1, width), BF16),
        ),
        in_specs=[left] * 14,
        out_specs=(vmem, vmem),
        scratch_shapes=[
            pltpu.SMEM(home_device.shape, home_device.dtype),
            pltpu.SMEM(lengths.shape, lengths.dtype),
            like(residual),
            pltpu.VMEM((1, width), F32),
            pltpu.VMEM((1, width), F32),
            pltpu.VMEM((feat,), F32),
            like(key_cache),
            like(value_cache),
            like(out_weight),
            pltpu.VMEM((hidden, width), BF16),
            pltpu.VMEM((hidden, width), BF16),
            pltpu.VMEM((hidden, width), BF16),
            pltpu.VMEM((feat, width), BF16),
            pltpu.VMEM((width, hidden), BF16),
            pltpu.VMEM((width, hidden), BF16),
            pltpu.VMEM((width, feat), BF16),
            pltpu.VMEM((1, width), BF16),
            pltpu.VMEM((HQ, HEAD), F32),
            pltpu.VMEM((n, HQ, HEAD), BF16),
            pltpu.VMEM((seqs, KVH, 8, HEAD), F32),
            pltpu.VMEM((seqs, width), F32),
            pltpu.VMEM((8, LANES), F32),
            pltpu.VMEM((n, seqs, win + LANES), BF16),
            pltpu.VMEM((n, seqs, win + LANES), BF16),
            pltpu.VMEM((1, seqs, width), BF16),
            pltpu.VMEM((n, seqs, win), BF16),
            pltpu.VMEM((seqs, win), BF16),
            pltpu.VMEM((n * share, seqs, win), BF16),
            pltpu.VMEM((share, seqs, width), BF16),
            pltpu.VMEM((n * share, seqs, win), BF16),
            pltpu.VMEM((seqs, win), BF16),
            pltpu.VMEM((n, seqs, win), BF16),
            pltpu.VMEM((n, 1, win), BF16),
            pltpu.VMEM((n, 1, win), BF16),
            pltpu.VMEM((len(plan.offsets), seqs, win), F32),
            pltpu.VMEM((seqs, win), F32),
            pltpu.VMEM((seqs * share, plan.chunk), F32),
            dma((14,)),
            dma((7,)),
            dma((7, plan.chunks)),
        ],
        compiler_params=pltpu.CompilerParams(
            collective_id=0, has_side_effects=True, vmem_limit_bytes=67043328
        ),
        name="decode_step",
    )(
        home_device,
        lengths,
        query_bias,
        queries,
        residual,
        ffn_gain[None, :],
        query_gain[None, :],
        key_cache,
        value_cache,
        out_weight,
        gate_weight.T,
        up_weight.T,
        down_weight,
        query_weight.T,
    )

    def hand_on(source_a, source_b, target_a, target_b, held_a, held_b, sem):
        copies = [
            pltpu.make_async_copy(source_b, held_b, sem.at[0]),
            pltpu.make_async_copy(source_a, held_a, sem.at[1]),
            pltpu.make_async_copy(held_b, target_b, sem.at[2]),
            pltpu.make_async_copy(held_a, target_a, sem.at[3]),
        ]
        copies[0].start()
        copies[1].start()
        copies[0].wait()
        copies[2].start()
        copies[1].wait()
        copies[3].start()
        copies[2].wait()
        copies[3].wait()

    return pl.pallas_call(
        hand_on,
        out_shape=(
            jax.ShapeDtypeStruct((seqs, feat), BF16),
            jax.ShapeDtypeStruct((1, width), BF16),
        ),
        in_specs=[left] * 2,
        out_specs=(left, left),
        scratch_shapes=[
            pltpu.VMEM((seqs, feat), BF16),
            pltpu.VMEM((1, width), BF16),
            dma((4,)),
        ],
        name="hand_on",
    )(leaving, asking)


def solution(mesh):
    placed = (
        P(("grp", "blk"), None),
        P("grp"),
        P("grp"),
        P("grp", "blk", None),
        P("grp", "blk", None),
        P("grp", "blk"),
        P("blk", None),
        P(),
        P(None, "blk"),
        P(None, "blk"),
        P("blk", None),
        P(),
        P(None, "blk"),
        P("blk"),
    )
    return jax.shard_map(
        functools.partial(local, mesh.shape["blk"], mesh.shape["grp"]),
        mesh=mesh,
        in_specs=placed,
        out_specs=(P("grp", "blk"), P(("grp", "blk"), None)),
        check_vma=False,
    )
```

```python
import functools
import math

import jax
import jax.numpy as jnp
from jax import lax
from jax.experimental import pallas as pl
from jax.experimental.pallas import tpu as pltpu
from jax.sharding import PartitionSpec as P

HQ = 40
KVH = 8
HEAD = 128
LANES = 128
GROUP = HQ // KVH
MESH = pl.DeviceIdType.MESH
F32 = jnp.float32
BF16 = jnp.bfloat16

ASK, MERGE, SUM_A, ROW_A, SUM_B, ROW_B, HOME = range(7)


class Plan:
    def __init__(self, n, width, wanted):
        self.n = n
        self.width = width
        self.feat = width // n
        unit = math.lcm(self.feat, LANES)
        self.chunk = unit
        while self.chunk * 2 <= wanted and width % (self.chunk * 2) == 0:
            self.chunk *= 2
        self.chunks = width // self.chunk
        self.per = self.chunk // self.feat
        self.tiles = self.chunk // LANES
        starts = [j * self.feat for j in range(self.per)]
        self.span = max(pl.cdiv(s % LANES + self.feat, LANES) for s in starts)
        self.clamped = any(s // LANES > self.tiles - self.span for s in starts)
        self.win = self.span * LANES
        self.first = [min(s // LANES, self.tiles - self.span) for s in starts]
        self.offsets = sorted({s - f * LANES for s, f in zip(starts, self.first)})

    def first_of(self, j):
        first = (j * self.feat) // LANES
        return jnp.minimum(first, self.tiles - self.span) if self.clamped else first


def dot_rows(left, right):
    return lax.dot_general(
        left, right, (((1,), (1,)), ((), ())), preferred_element_type=F32
    )


def kernel(
    plan,
    share,
    groups,
    home_hbm,
    length_hbm,
    bias_hbm,
    queries,
    residual_hbm,
    ffn_gain_hbm,
    query_gain_hbm,
    key_hbm,
    value_hbm,
    out_hbm,
    gate_hbm,
    up_hbm,
    down_hbm,
    query_hbm,
    hidden_out,
    next_out,
    home,
    length,
    residual,
    ffn_gain,
    query_gain,
    query_bias,
    keys,
    values,
    out_w,
    gate_w,
    up_w,
    down_w,
    query_w,
    gate_t,
    up_t,
    query_t,
    line,
    lined,
    asked,
    heads,
    flat,
    stats,
    merge_send,
    merge_recv,
    sum_a_send,
    sum_a_recv,
    row_a_send,
    row_a_recv,
    sum_b_send,
    sum_b_recv,
    row_b_send,
    row_b_recv,
    home_send,
    home_recv,
    shifted,
    taken,
    wide,
    load_sem,
    send_sem,
    recv_sem,
):
    n, feat, width = plan.n, plan.feat, plan.width
    chunk, chunks, per, tiles = plan.chunk, plan.chunks, plan.per, plan.tiles
    win = plan.win
    me = lax.axis_index("blk")
    grp = lax.axis_index("grp")
    seqs = residual.shape[0]
    span = keys.shape[1]
    my_chunk = me // per
    my_place = lax.rem(me, per)
    hidden = gate_w.shape[0]
    shard = grp if share > 1 else 0
    half = pl.ds(pl.multiple_of(shard * hidden, 16), hidden)

    def load(src, dst, i):
        return pltpu.make_async_copy(src, dst, load_sem.at[i])

    loads = [
        load(src, dst, i)
        for i, (src, dst) in enumerate(
            (
                (queries, line),
                (home_hbm, home),
                (length_hbm, length),
                (key_hbm, keys),
                (value_hbm, values),
                (residual_hbm, residual),
                (gate_hbm.at[half], gate_w),
                (up_hbm.at[half], up_w),
                (out_hbm, out_w),
                (ffn_gain_hbm, ffn_gain),
                (down_hbm.at[half], down_w),
                (query_gain_hbm, query_gain),
                (query_hbm, query_w),
                (bias_hbm, query_bias),
            )
        )
    ]
    ASKED, HOMES, LENGTHS, KEYS, VALUES, REST, GATE, UP, OUT, GAIN_A, DOWN, GAIN_B, QUERY, BIAS = range(14)

    def each(low, high, action, unroll=True):
        def body(i, carry):
            action(i)
            return carry

        lax.fori_loop(low, high, body, 0, unroll=unroll)

    def remote(phase, source, target, sem, g, peer):
        pltpu.make_async_remote_copy(
            src_ref=source,
            dst_ref=target,
            send_sem=send_sem.at[phase],
            recv_sem=sem,
            device_id={"grp": g, "blk": peer},
            device_id_type=MESH,
        ).start()

    def start(phase, source, target):
        for c in reversed(range(chunks)):
            reach(
                c,
                1,
                lambda g, peer, j, at: remote(
                    phase, source(peer), target.at[me], recv_sem.at[phase, 0], g, peer
                ),
            )

    def await_bytes(sem, target, count):
        part = target.at[pl.ds(0, count)]
        pltpu.make_async_copy(part, part, sem).wait()

    def slot(parts, g, peer):
        if parts == 1:
            return peer
        return (peer // per) * (parts * per) + g * per + lax.rem(peer, per)

    def partner(c):
        if chunks & (chunks - 1):
            return lax.rem(my_chunk + c, chunks)
        at, bit = my_chunk, 1
        while bit < chunks:
            if c & bit:
                at = at + bit - 2 * bit * lax.rem(my_chunk // bit, 2)
            bit *= 2
        return at

    def reach(c, parts, action):
        at = partner(c)

        def one(i):
            g = lax.rem(grp + parts - 1 - i // per, parts) if parts > 1 else grp
            j = lax.rem(my_place + i, per)
            action(g, at * per + j, j, at)

        skip = (parts - 1) * per
        if c:
            each(0, parts * per, one)
        else:
            if parts > 1:
                each(0, skip, one)
            each(skip + 1, parts * per, one)

    barrier = pltpu.get_barrier_semaphore()

    def greet(g, peer, j, at):
        pl.semaphore_signal(
            barrier, inc=1, device_id={"grp": g, "blk": peer}, device_id_type=MESH
        )

    for c in reversed(range(chunks)):
        reach(c, share, greet)
    for one in loads:
        one.start()

    def turn(source, target, block):
        def one(i):
            at = pl.ds(pl.multiple_of(i * block, block), block)
            target[at, :] = source[:, at].T

        each(0, width // block, one, 1)

    heads[...] = jnp.zeros_like(heads)
    stats[...] = jnp.zeros_like(stats)
    shifted[...] = jnp.zeros_like(shifted)

    my_first = plan.first_of(my_place)
    offset = my_place * feat - my_first * LANES
    lane = lax.broadcasted_iota(jnp.int32, (seqs, win), 1)
    mine = (lane >= offset) & (lane < offset + feat)

    def narrow(value):
        taken[...] = value
        found = taken[:, plan.offsets[0] : plan.offsets[0] + feat]
        for o in plan.offsets[1:]:
            found = jnp.where(offset == o, taken[:, o : o + feat], found)
        return found

    def widen(value):
        for i, o in enumerate(plan.offsets):
            shifted[i, :, o : o + feat] = value
        found = shifted[0]
        for i, o in enumerate(plan.offsets[1:]):
            found = jnp.where(offset == o, shifted[i + 1], found)
        return found

    loads[ASKED].wait()
    whole_line = line[...].astype(F32)
    for h in range(HQ):
        lined[pl.ds(h, 1), :] = whole_line[:, h * HEAD : (h + 1) * HEAD]
    asked[me] = lined[...].astype(BF16)
    pl.semaphore_wait(barrier, n * share - 1)
    start(ASK, lambda peer: asked.at[me], asked)
    loads[HOMES].wait()
    loads[LENGTHS].wait()
    loads[REST].wait()
    resting = widen(residual[...].astype(F32))
    loads[KEYS].wait()
    loads[VALUES].wait()

    pad = 8
    rows = KVH * pad
    position = me * span + lax.broadcasted_iota(jnp.int32, (rows, span), 1)
    at_row = lax.broadcasted_iota(jnp.int32, (rows, LANES), 0)
    at_lane = lax.broadcasted_iota(jnp.int32, (rows, LANES), 1)
    row_head = (at_row // pad) * GROUP + lax.rem(at_row, pad)
    real = lax.rem(at_row, pad) < GROUP
    loads[GATE].wait()
    turn(gate_w, gate_t, 512)
    await_bytes(recv_sem.at[ASK, 0], asked, n - 1)
    for s in range(seqs):
        asking = asked[home[s]].astype(F32)
        for k in range(KVH):
            heads[s, k, 0:GROUP, :] = asking[k * GROUP : (k + 1) * GROUP]
    scores = [
        jnp.concatenate(
            [
                dot_rows(heads[s, k].astype(BF16), keys[s, :, k * HEAD : (k + 1) * HEAD])
                for k in range(KVH)
            ],
            axis=0,
        ) * HEAD ** (-0.5)
        for s in range(seqs)
    ]
    allowed = [position < length[s] for s in range(seqs)]
    masked = [jnp.where(allowed[s], scores[s], -1e30) for s in range(seqs)]
    peaks = [
        jnp.max(masked[s], axis=1, keepdims=True).astype(BF16).astype(F32) for s in range(seqs)
    ]
    raised = [
        jnp.where(allowed[s], jnp.exp(masked[s] - peaks[s]), 0.0) for s in range(seqs)
    ]
    for s in range(seqs):
        for k in range(KVH):
            mixed = jnp.dot(
                raised[s][k * pad : (k + 1) * pad].astype(BF16),
                values[s, :, k * HEAD : (k + 1) * HEAD],
                preferred_element_type=F32,
            )
            for g in range(GROUP):
                h = k * GROUP + g
                flat[pl.ds(s, 1), h * HEAD : (h + 1) * HEAD] = mixed[g : g + 1]
    for s in range(seqs):
        total = jnp.sum(raised[s], axis=1, keepdims=True)
        high = total.astype(BF16).astype(F32)
        spread = jnp.where(at_lane == row_head, peaks[s], 0.0)
        spread = spread + jnp.where(at_lane == row_head + HQ, high, 0.0)
        spread = spread + jnp.where(at_lane == row_head + 2 * HQ, total - high, 0.0)
        stats[pl.ds(s, 1), :] = jnp.sum(jnp.where(real, spread, 0.0), axis=0, keepdims=True)

    noted = stats[...]
    for d in range(n):
        tile = (d // per) * tiles + plan.first[d % per]
        merge_send[d, :, 0:win] = flat[:, tile * LANES : tile * LANES + win].astype(BF16)
        rolled = pltpu.roll(noted, (LANES - tile) % LANES, 1) if tile else noted
        merge_send[d, :, win : win + LANES] = rolled[0:seqs].astype(BF16)
    start(MERGE, lambda peer: merge_send.at[peer], merge_recv)
    merge_recv[me] = merge_send[me]
    loads[UP].wait()
    turn(up_w, up_t, 512)
    loads[OUT].wait()
    await_bytes(recv_sem.at[MERGE, 0], merge_recv, n - 1)

    stat = merge_recv[:, :, win : win + LANES].astype(F32)
    scale = jnp.exp(stat - jnp.max(stat, axis=0, keepdims=True))
    flat_stat = stat.reshape(n * seqs, LANES)
    whole = pltpu.roll(flat_stat, LANES - HQ, 1) + pltpu.roll(flat_stat, LANES - 2 * HQ, 1)
    whole = whole.reshape(n, seqs, LANES)
    factors = scale / jnp.sum(scale * whole, axis=0, keepdims=True)
    blended = []
    for t in range(plan.span):
        part = merge_recv[:, :, t * LANES : (t + 1) * LANES].astype(F32)
        blended.append(jnp.sum(part * factors[:, :, t : t + 1], axis=0))
    context = narrow(jnp.concatenate(blended, axis=1)).astype(BF16)

    def window(at, j):
        return pl.ds(pl.multiple_of(at * chunk + plan.first_of(j) * LANES, LANES), win)

    def cols_of(c):
        at = partner(c)
        return pl.ds(pl.multiple_of(at * chunk, chunk), chunk)

    def scatter(phase, parts, product, source, target, meanwhile):
        own = slot(parts, grp, me)
        for c in reversed(range(chunks)):
            cols = cols_of(c)
            made = product(cols)
            for g in range(parts):
                source[g, :, cols] = made[g * seqs : (g + 1) * seqs].astype(BF16)

            def send(g, peer, j, at):
                remote(
                    phase,
                    source.at[g if parts > 1 else 0, :, window(at, j)],
                    target.at[own],
                    recv_sem.at[phase, 0],
                    g,
                    peer,
                )

            reach(c, parts, send)
        target[own] = source[grp if parts > 1 else 0, :, window(my_chunk, my_place)]
        meanwhile()
        await_bytes(recv_sem.at[phase, 0], target, n * parts - 1)
        return jnp.sum(target[...].astype(F32), axis=0)

    def spread_rows(phase, parts, value, source, target):
        own = slot(parts, grp, me)
        source[...] = value
        for c in [0, *reversed(range(1, chunks))]:
            reach(
                c,
                parts,
                lambda g, peer, j, at: remote(
                    phase, source, target.at[own], recv_sem.at[phase, my_chunk], g, peer
                ),
            )
        target[own] = value

    def gathered(phase, parts, target, c):
        at = partner(c)
        await_bytes(recv_sem.at[phase, at], target, parts * per - (c == 0))
        base = at * (parts * per)
        for g in range(parts):
            for t in range(tiles):
                whole = None
                for j in range(per):
                    k = t - plan.first[j]
                    if 0 <= k < plan.span:
                        piece = target[base + g * per + j, :, k * LANES : (k + 1) * LANES].astype(F32)
                        whole = piece if whole is None else whole + piece
                wide[g * seqs : (g + 1) * seqs, t * LANES : (t + 1) * LANES] = whole
        return wide[0 : parts * seqs, :]

    def normed(phase, parts, target, gain, matrices):
        sums = [None] * len(matrices)
        square = None
        for c in range(chunks):
            cols = cols_of(c)
            row = gathered(phase, parts, target, c)
            piece = (row * gain[:, cols]).astype(BF16)
            found = row * row
            square = found if square is None else square + found
            for i, matrix in enumerate(matrices):
                part = jnp.dot(piece, matrix[cols, :], preferred_element_type=F32)
                sums[i] = part if sums[i] is None else sums[i] + part
        mean = jnp.sum(square, axis=1, keepdims=True) * (1.0 / width)
        root = lax.rsqrt(mean + 1e-06)
        return [total * root for total in sums]

    def turn_query():
        loads[QUERY].wait()
        turn(query_w, query_t, 512)

    total = scatter(
        SUM_A,
        1,
        lambda cols: jnp.dot(context, out_w[:, cols], preferred_element_type=F32),
        sum_a_send,
        sum_a_recv,
        turn_query,
    )
    carried = jnp.where(mine, resting + total, 0.0).astype(BF16)
    spread_rows(ROW_A, share, carried, row_a_send, row_a_recv)
    loads[GAIN_A].wait()
    gate, up = normed(ROW_A, share, row_a_recv, ffn_gain, (gate_t, up_t))
    activated = (gate / (1.0 + jnp.exp(-gate)) * up).astype(BF16)

    loads[DOWN].wait()
    total = scatter(
        SUM_B,
        share,
        lambda cols: jnp.dot(activated, down_w[:, cols], preferred_element_type=F32),
        sum_b_send,
        sum_b_recv,
        lambda: None,
    )
    leaving = jnp.where(mine, carried.astype(F32) + total, 0.0).astype(BF16)
    spread_rows(ROW_B, 1, leaving, row_b_send, row_b_recv)
    hidden_out[...] = narrow(leaving.astype(F32)).astype(BF16)
    loads[GAIN_B].wait()
    loads[BIAS].wait()
    (fresh,) = normed(ROW_B, 1, row_b_recv, query_gain, (query_t,))
    fresh = (fresh + query_bias[...][None, :]).astype(BF16).astype(F32)
    fresh = widen(fresh)

    device = lax.broadcasted_iota(jnp.int32, (n, win), 0)
    lines = jnp.zeros((n, win), F32)
    for s in range(seqs):
        lines = lines + jnp.where(device == home[s], fresh[s : s + 1], 0.0)
    for d in range(n):
        home_send[d] = lines[d : d + 1].astype(BF16)
    start(HOME, lambda peer: home_send.at[peer], home_recv)
    home_recv[me] = home_send[me]
    await_bytes(recv_sem.at[HOME, 0], home_recv, n - 1)
    for t in range(width // LANES):
        whole = None
        for j in range(per):
            k = t % tiles - plan.first[j]
            if 0 <= k < plan.span:
                d = (t // tiles) * per + j
                piece = home_recv[d, :, k * LANES : (k + 1) * LANES].astype(F32)
                whole = piece if whole is None else whole + piece
        next_out[:, t * LANES : (t + 1) * LANES] = whole.astype(BF16)

    await_bytes(send_sem.at[ASK], asked, n - 1)
    await_bytes(send_sem.at[MERGE], merge_recv, n - 1)
    await_bytes(send_sem.at[SUM_A], sum_a_recv, n - 1)
    await_bytes(send_sem.at[ROW_A], row_a_recv, n * share - 1)
    await_bytes(send_sem.at[SUM_B], sum_b_recv, n * share - 1)
    await_bytes(send_sem.at[ROW_B], row_b_recv, n - 1)
    await_bytes(send_sem.at[HOME], home_recv, n - 1)


def local(
    n,
    groups,
    queries,
    home_device,
    lengths,
    key_cache,
    value_cache,
    residual,
    out_weight,
    ffn_gain,
    gate_weight,
    up_weight,
    down_weight,
    query_gain,
    query_weight,
    query_bias,
):
    seqs, feat = residual.shape
    width = queries.shape[1]
    hidden = gate_weight.shape[1]
    share = groups if hidden % (16 * groups) == 0 else 1
    hidden //= share
    plan = Plan(n, width, 640)
    win = plan.win
    vmem = pl.BlockSpec(memory_space=pltpu.VMEM)
    left = pl.BlockSpec(memory_space=pl.ANY)
    dma = pltpu.SemaphoreType.DMA

    def like(array):
        return pltpu.VMEM(array.shape, array.dtype)

    leaving, asking = pl.pallas_call(
        functools.partial(kernel, plan, share, groups),
        out_shape=(
            jax.ShapeDtypeStruct((seqs, feat), BF16),
            jax.ShapeDtypeStruct((1, width), BF16),
        ),
        in_specs=[left] * 14,
        out_specs=(vmem, vmem),
        scratch_shapes=[
            pltpu.SMEM(home_device.shape, home_device.dtype),
            pltpu.SMEM(lengths.shape, lengths.dtype),
            like(residual),
            pltpu.VMEM((1, width), F32),
            pltpu.VMEM((1, width), F32),
            pltpu.VMEM((feat,), F32),
            like(key_cache),
            like(value_cache),
            like(out_weight),
            pltpu.VMEM((hidden, width), BF16),
            pltpu.VMEM((hidden, width), BF16),
            pltpu.VMEM((hidden, width), BF16),
            pltpu.VMEM((feat, width), BF16),
            pltpu.VMEM((width, hidden), BF16),
            pltpu.VMEM((width, hidden), BF16),
            pltpu.VMEM((width, feat), BF16),
            pltpu.VMEM((1, width), BF16),
            pltpu.VMEM((HQ, HEAD), F32),
            pltpu.VMEM((n, HQ, HEAD), BF16),
            pltpu.VMEM((seqs, KVH, 8, HEAD), F32),
            pltpu.VMEM((seqs, width), F32),
            pltpu.VMEM((8, LANES), F32),
            pltpu.VMEM((n, seqs, win + LANES), BF16),
            pltpu.VMEM((n, seqs, win + LANES), BF16),
            pltpu.VMEM((1, seqs, width), BF16),
            pltpu.VMEM((n, seqs, win), BF16),
            pltpu.VMEM((seqs, win), BF16),
            pltpu.VMEM((n * share, seqs, win), BF16),
            pltpu.VMEM((share, seqs, width), BF16),
            pltpu.VMEM((n * share, seqs, win), BF16),
            pltpu.VMEM((seqs, win), BF16),
            pltpu.VMEM((n, seqs, win), BF16),
            pltpu.VMEM((n, 1, win), BF16),
            pltpu.VMEM((n, 1, win), BF16),
            pltpu.VMEM((len(plan.offsets), seqs, win), F32),
            pltpu.VMEM((seqs, win), F32),
            pltpu.VMEM((seqs * share, plan.chunk), F32),
            dma((14,)),
            dma((7,)),
            dma((7, plan.chunks)),
        ],
        compiler_params=pltpu.CompilerParams(
            collective_id=0, has_side_effects=True, vmem_limit_bytes=67043328
        ),
        name="decode_step",
    )(
        home_device,
        lengths,
        query_bias,
        queries,
        residual,
        ffn_gain[None, :],
        query_gain[None, :],
        key_cache,
        value_cache,
        out_weight,
        gate_weight.T,
        up_weight.T,
        down_weight,
        query_weight.T,
    )

    def hand_on(source_a, source_b, target_a, target_b, held_a, held_b, sem):
        copies = [
            pltpu.make_async_copy(source_b, held_b, sem.at[0]),
            pltpu.make_async_copy(source_a, held_a, sem.at[1]),
            pltpu.make_async_copy(held_b, target_b, sem.at[2]),
            pltpu.make_async_copy(held_a, target_a, sem.at[3]),
        ]
        copies[0].start()
        copies[1].start()
        copies[0].wait()
        copies[2].start()
        copies[1].wait()
        copies[3].start()
        copies[2].wait()
        copies[3].wait()

    return pl.pallas_call(
        hand_on,
        out_shape=(
            jax.ShapeDtypeStruct((seqs, feat), BF16),
            jax.ShapeDtypeStruct((1, width), BF16),
        ),
        in_specs=[left] * 2,
        out_specs=(left, left),
        scratch_shapes=[
            pltpu.VMEM((seqs, feat), BF16),
            pltpu.VMEM((1, width), BF16),
            dma((4,)),
        ],
        name="hand_on",
    )(leaving, asking)


def solution(mesh):
    placed = (
        P(("grp", "blk"), None),
        P("grp"),
        P("grp"),
        P("grp", "blk", None),
        P("grp", "blk", None),
        P("grp", "blk"),
        P("blk", None),
        P(),
        P(None, "blk"),
        P(None, "blk"),
        P("blk", None),
        P(),
        P(None, "blk"),
        P("blk"),
    )
    return jax.shard_map(
        functools.partial(local, mesh.shape["blk"], mesh.shape["grp"]),
        mesh=mesh,
        in_specs=placed,
        out_specs=(P("grp", "blk"), P(("grp", "blk"), None)),
        check_vma=False,
    )
```
